128 devices in a mesh: lat: 4 (over y), lon: 32 (over x, z, core).
Axes of the slice: x: 4, y: 4, z: 4, core: 2. Of those that a mesh axis runs over, the one named last changes fastest.
Arguments:
- conc: bfloat16 [128, 64, 8192], P('lat', None, 'lon'), may hold values from -6 to 6
- dep_owner: int32 [32, 128, 4], P('lon', 'lat'), may hold values from 0 to 14, all different within a row; in each aligned block of 32 rows (0 to 31, 32 to 63, ..., all dimensions but the last counted through in order) at most 17 rows name the same one
- dep_row: int32 [32, 128, 4], P('lon', 'lat'), may hold values from 0 to 31
- dep_weight: float32 [32, 128, 4], P('lon', 'lat'), may hold values from 0.05 to 0.5
- dep_count: int32 [32, 128], P('lon', 'lat'), may hold values from 1 to 4
- zonal_offset: int32 [128], P('lat'), may hold values from -2 to 2
- agg_rates: float32 [4, 128, 8192], P(None, 'lat', 'lon'), may hold values from 0.1 to 1
- toeplitz: bfloat16 [4, 127], replicated, may hold values from -0.75 to 0.75
- settle: float32 [64], replicated, may hold values from 0.05 to 0.5
- kappa: float32 [128, 8192], P('lat', 'lon'), may hold values from 0.02 to 0.2
Outputs:
- updated: float32 [128, 64, 8192], P('lat', None, 'lon')
The draws below stay inside these ranges and needn't reach their ends.
Inputs may be any that keep to these rules, and one draw needn't show every extreme that they name: `dep_owner`: the 4 entries of a row name different neighbour blocks; among the rows of one device no neighbour block is named by more than 17 entries, and in some device's rows one is named exactly 17 times; every value is named somewhere. `dep_count`: entries of a row at or past its count are padding.
All inputs are finite; a program needn't handle non-finite values.
Results may differ from the reference program's by a relative error of at most 0.00092.
Values may be sent and summed in bfloat16 or wider, within the bound.
A program may use at most 64 MiB of HBM per device.

```python
import math
import jax
import jax.numpy as jnp
import numpy as np
from jax import lax

B = 64
RANK = 4
KS = 4
NEAR = 15
LAT_DEV = 32
LON_DEV = 256
LAT = 128
NLON = 8192
CAP = 17
N_LAT = 4
N_LON = 32


def with_ends(values, own_key, low, top_value):
    index_at = [jax.random.randint(jax.random.fold_in(own_key, axis), (), 0, length) for axis, length in enumerate(values.shape)]
    widest = values.shape.index(max(values.shape))
    beside = index_at[:widest] + [(index_at[widest] + 1) % values.shape[widest]] + index_at[widest + 1:]
    return values.at[tuple(index_at)].set(low).at[tuple(beside)].set(top_value)


def block_levels(key, dims, shards, least, top_value):
    level = 1.0
    for position, blocks in shards:
        steps = jax.random.uniform(jax.random.fold_in(jax.random.fold_in(key, 6), position), (blocks,), jnp.float32, least / len(shards), top_value / len(shards))
        level = level * jnp.repeat(jnp.exp(steps), dims[position] // blocks).reshape((-1,) + (1,) * (len(dims) - 1 - position))
    return level


def assign_block(own_key, own, number, rows, amount, top, bound, skew):
    order = jax.random.permutation(own_key, amount)
    crowded, common = portions_of(amount, rows * top, bound, skew, True), portions_of(amount, rows * top, bound, skew, False)
    places = jnp.arange(amount)

    def named(lengths, rotation):
        used = int((lengths > 0).sum())
        fixed = max(1, used // 4)
        passed = fixed + (places - fixed + rotation * (used - fixed)) % max(1, amount - fixed)
        return jnp.zeros((amount,), jnp.int32).at[order[jnp.where(places < fixed, places, passed)]].set(jnp.asarray(lengths, jnp.int32))

    lengths = jnp.where(number % 4 == 0, named(crowded, number // 4), named(common, number - number // 4 - 1))
    mixed = jax.random.permutation(jax.random.fold_in(own, 3), amount)
    source_of, receiver = mixed[0:amount // 2 * 2:2], mixed[1:amount // 2 * 2:2]
    room = jnp.minimum(lengths[source_of] - 1, bound - lengths[receiver]) // 2
    room = jnp.where((source_of == order[0]) | (receiver == order[0]) | (lengths[receiver] == 0), 0, jnp.maximum(room, 0))
    passed = jax.random.randint(jax.random.fold_in(own, 4), (amount // 2,), 0, 1 << 20) % (room + 1)
    lengths = lengths.at[source_of].add(-passed).at[receiver].add(passed)
    items = jnp.searchsorted(jnp.cumsum(lengths), jnp.arange(rows * top), side="right").astype(jnp.int32)
    grid = items.reshape(top, rows).T
    grid = grid[jax.random.permutation(jax.random.fold_in(own, 1), rows)]
    rotation = jax.random.randint(jax.random.fold_in(own, 2), (rows, 1), 0, top)
    return jnp.take_along_axis(grid, (jnp.arange(top)[None, :] + rotation) % top, axis=1)


def portions_of(amount, total, limit, skew, full):
    weights = [(1 << 20) // math.isqrt(standing ** skew) + 1 for standing in range(1, amount + 1)]
    largest = limit if full else min(limit, max(-(-total // amount), total * weights[0] // sum(weights)))
    least = 1 if total - largest >= amount - 1 else 0
    counts, spare = [largest] + [least] * (amount - 1), total - largest - least * (amount - 1)
    while spare > 0:
        movable = [i for i in range(1, amount) if counts[i] < largest] or [i for i in range(1, amount) if counts[i] < limit]
        whole, budget = sum([weights[i] for i in movable]), spare
        for i in movable:
            more = min(limit - counts[i], max(1, budget * weights[i] // whole), spare)
            counts[i] = counts[i] + more
            spare = spare - more
    return np.array(counts)


def scatter_about(rng, extent, width, bound, cuts=(), held_as=jnp.bfloat16):
    drawn = width * jax.random.normal(rng, extent, jnp.float32)
    if cuts:
        drawn = drawn * block_levels(rng, extent, cuts, -0.22, 0.18)
    return jnp.clip(drawn, -bound, bound).astype(held_as)


def setup_inputs(seed: int = 0) -> dict:
    streams_of = jax.random.split(jax.random.key(seed), 11)
    conc = scatter_about(streams_of[0], (LAT, B, NLON), 1.0, 6.0, ((0, 4), (2, 32)))
    dep_owner_keys = jax.random.split(jax.random.fold_in(streams_of[1], 1), N_LON * LAT // LAT_DEV)
    dep_owner_turns = jax.random.permutation(jax.random.fold_in(streams_of[1], 3), N_LON * LAT // LAT_DEV)
    dep_owner = jax.vmap(lambda own, number: assign_block(jax.random.fold_in(streams_of[1], 2), own, number, LAT_DEV, NEAR, KS, CAP, 2))(dep_owner_keys, dep_owner_turns).reshape((N_LON, LAT, KS))
    dep_row = with_ends(jax.random.randint(streams_of[2], (N_LON, LAT, KS), 0, LAT_DEV), jax.random.fold_in(streams_of[2], 1), 0, LAT_DEV - 1).astype(jnp.int32)
    dep_weight = jnp.clip(0.05 + 0.45 * jax.random.uniform(streams_of[3], (N_LON, LAT, KS), jnp.float32) ** block_levels(streams_of[3], (N_LON, LAT, KS), ((0, 32), (1, 4)), -0.2, 0.2), 0.05, 0.5)
    dep_count = with_ends(jax.random.randint(streams_of[4], (N_LON, LAT), 1, KS + 1), jax.random.fold_in(streams_of[4], 1), 1, KS).astype(jnp.int32)
    zonal_offset = with_ends(jax.random.randint(streams_of[5], (LAT,), -2, 3), jax.random.fold_in(streams_of[5], 1), -2, 2).astype(jnp.int32)
    agg_rates = jnp.clip(jnp.exp(math.log(1.0) - 2.3025851 * jax.random.uniform(streams_of[6], (RANK, LAT, NLON), jnp.float32) ** block_levels(streams_of[6], (RANK, LAT, NLON), ((1, 4), (2, 32)), -0.2, 0.2)), 0.1, 1.0)
    toeplitz = scatter_about(streams_of[7], (RANK, 2 * B - 1), B ** -0.5, 0.75)
    settle = jnp.clip(jnp.exp(jax.random.uniform(streams_of[8], (B,), jnp.float32, math.log(0.05), math.log(0.5))), 0.05, 0.5)
    kappa = jnp.clip(jnp.exp(math.log(0.2) - 2.3025851 * jax.random.uniform(streams_of[9], (LAT, NLON), jnp.float32) ** block_levels(streams_of[9], (LAT, NLON), ((0, 4), (1, 32)), -0.2, 0.2)), 0.02, 0.2)
    return dict(conc=conc, dep_owner=dep_owner, dep_row=dep_row, dep_weight=dep_weight, dep_count=dep_count, zonal_offset=zonal_offset, agg_rates=agg_rates, toeplitz=toeplitz, settle=settle, kappa=kappa)


def toeplitz_stack(toeplitz, bins):
    flipped = toeplitz[:, ::-1]
    return jnp.stack([flipped[:, bins - 1 - i: 2 * bins - 1 - i] for i in range(bins)], axis=1)


def reference(conc, dep_owner, dep_row, dep_weight, dep_count, zonal_offset, agg_rates, toeplitz, settle, kappa):
    band_field = conc.reshape(LAT, B, N_LON, LON_DEV)
    entry_ids = jnp.arange(KS, dtype=jnp.int32)
    lat_block = (jnp.arange(LAT, dtype=jnp.int32) // LAT_DEV).astype(jnp.int32)

    def remap_block(inputs):
        block_index, owner, source_row, weight, count = inputs
        source_block = (lat_block[:, None] + owner // 5 - 1).astype(jnp.int32)
        inside = (source_block >= 0) & (source_block < N_LAT)
        source_lat = jnp.clip(source_block * LAT_DEV + source_row, 0, LAT - 1).astype(jnp.int32)
        source_lon = ((block_index + owner % 5 - 2) % N_LON).astype(jnp.int32)
        keep = (entry_ids[None, :] < count[:, None]) & inside
        live_weight = jnp.where(keep, weight, jnp.float32(0.0))
        summed = jnp.zeros((LAT, B, LON_DEV), jnp.float32)
        for k in range(KS):
            row_data = band_field[source_lat[:, k], :, source_lon[:, k], :]
            summed = summed + live_weight[:, k, None, None] * row_data.astype(jnp.float32)
        return summed.astype(jnp.bfloat16)

    block_ids = jnp.arange(N_LON, dtype=jnp.int32)
    blocks = lax.map(remap_block, (block_ids, dep_owner, dep_row, dep_weight, dep_count))
    remapped = jnp.transpose(blocks, (1, 2, 0, 3)).reshape(LAT, B, NLON)
    displace = zonal_offset[:, None, None]
    shifted = jnp.zeros_like(remapped)
    for step in range(-2, 3):
        shifted = shifted + jnp.where(displace == step, jnp.roll(remapped, step, axis=2), jnp.zeros_like(remapped))
    center = shifted.astype(jnp.float32)
    padded = jnp.pad(center, ((1, 1), (0, 0), (0, 0)))
    neighbours = padded[2:] + padded[:-2] + jnp.roll(center, -1, axis=2) + jnp.roll(center, 1, axis=2)
    diffusion = kappa[:, None, :] * (neighbours - 4.0 * center)
    matrices = toeplitz_stack(toeplitz, B).astype(jnp.float32)
    conc_wide = conc.astype(jnp.float32)
    growth = jnp.zeros((LAT, B, NLON), jnp.float32)
    for q in range(RANK):
        growth = growth + agg_rates[q][:, None, :] * jnp.einsum("ij,ljx->lix", matrices[q], conc_wide)
    return center + diffusion + growth - settle[None, :, None] * conc_wide
```

```python
import functools

import jax
import jax.numpy as jnp
from jax import lax
from jax.experimental import pallas as pl
from jax.experimental.pallas import tpu as pltpu
from jax.sharding import PartitionSpec as P

MESH = pl.DeviceIdType.MESH
ROWS = 32
BINS = 64
WIDTH = 256
ENTRIES = 4
GROUP = 16
GROUPS = BINS // GROUP
HALVES = 1
LANES = WIDTH // HALVES
CHUNKS = GROUPS * HALVES
AHEAD = 2
STRIP = 128


def kernel(
    n_lat, n_lon,
    conc, owner_v, row_v, weight_v, count_v, owner_s, row_s, weight_s, count_s, offset_s,
    rates, toeplitz, settle, kappa,
    out,
    conc_v, base, taps, toep_v, near_int, near_weight, near_count,
    own_int, near_int_s, near_weight_s, near_count_s, index_s, mix_s, scale_s,
    *rest,
):
    held = rest[0:CHUNKS]
    sent = rest[CHUNKS:2 * CHUNKS]
    got = rest[2 * CHUNKS:3 * CHUNKS]
    remapped = rest[3 * CHUNKS:3 * CHUNKS + GROUPS]
    strips = rest[3 * CHUNKS + GROUPS:3 * CHUNKS + 2 * GROUPS]
    ends = rest[3 * CHUNKS + 2 * GROUPS:3 * CHUNKS + 3 * GROUPS]
    edges = rest[3 * CHUNKS + 3 * GROUPS:3 * CHUNKS + 4 * GROUPS]
    (dep_send, dep_recv, raw_send, raw_recv, part_send, part_recv,
     strip_send, strip_recv, edge_send, edge_recv, local_sem, out_sem) = rest[3 * CHUNKS + 4 * GROUPS:]

    lat = lax.axis_index("lat")
    lon = lax.axis_index("lon")
    core = lax.rem(lon, 2)
    chip = lon - core

    def at_lon(value):
        return lax.rem(value + 2 * n_lon, n_lon)

    sibling = chip + 1 - core
    after = at_lon(chip + 2)
    before = at_lon(chip - 1)
    west, east = at_lon(lon - 1), at_lon(lon + 1)

    barrier = pltpu.get_barrier_semaphore()
    for step in (-2, -1, 1, 2):
        pl.semaphore_signal(barrier, inc=1, device_id={"lon": at_lon(lon + step)}, device_id_type=MESH)

    def with_neighbour(side, action):
        inside = lat > 0 if side == 0 else lat < n_lat - 1
        pl.when(inside)(functools.partial(action, side, lat - 1 if side == 0 else lat + 1))

    def greet(side, there):
        pl.semaphore_signal(barrier, inc=1, device_id={"lat": there}, device_id_type=MESH)

    for side in (0, 1):
        with_neighbour(side, greet)
    pl.semaphore_wait(barrier, 4 + jnp.where(lat > 0, 1, 0) + jnp.where(lat < n_lat - 1, 1, 0))

    def remote(src, dst, send, recv, **where):
        return pltpu.make_async_remote_copy(
            src_ref=src, dst_ref=dst, send_sem=send, recv_sem=recv, device_id=where, device_id_type=MESH
        )

    def window(c):
        g, h = c // HALVES, c % HALVES
        return conc.at[:, pl.ds(g * GROUP, GROUP), pl.ds(h * LANES, LANES)]

    def slot(c, number):
        return held[c].at[pl.ds(number * ROWS, ROWS)]

    def raw_sends(c):
        return [
            remote(window(c), slot(c, core), raw_send.at[c, 0], raw_recv.at[c, core], lon=after),
            remote(window(c), slot(c, core + 3), raw_send.at[c, 1], raw_recv.at[c, core], lon=before),
            remote(window(c), slot(c, 1 + 2 * core), raw_send.at[c, 2], raw_recv.at[c, 2], lon=sibling),
        ]

    far = 3 * core

    def raw_arrival(c, which):
        number = (far, far + 1, 3 - 2 * core, 4 - 4 * core)[which]
        return remote(window(c), slot(c, number), raw_send.at[c, 3], raw_recv.at[c, which], lon=sibling)

    def forward(c):
        return remote(
            slot(c, 1 + 2 * core), slot(c, 4 * core), raw_send.at[c, 3], raw_recv.at[c, 3], lon=sibling
        )

    def own_copy(c):
        return pltpu.make_async_copy(window(c), slot(c, 2), local_sem.at[c])

    def dep_sends(side, there):
        other = 1 - side
        return [
            remote(owner_v, near_int.at[other, 0], dep_send.at[side, 0], dep_recv.at[other, 0], lat=there),
            remote(row_v, near_int.at[other, 1], dep_send.at[side, 1], dep_recv.at[other, 1], lat=there),
            remote(weight_v, near_weight.at[other], dep_send.at[side, 2], dep_recv.at[other, 2], lat=there),
            remote(count_v, near_count.at[other], dep_send.at[side, 3], dep_recv.at[other, 3], lat=there),
        ]

    def dep_arrivals(side, there):
        return [
            remote(owner_v, near_int.at[side, 0], dep_send.at[side, 0], dep_recv.at[side, 0], lat=there),
            remote(row_v, near_int.at[side, 1], dep_send.at[side, 1], dep_recv.at[side, 1], lat=there),
            remote(weight_v, near_weight.at[side], dep_send.at[side, 2], dep_recv.at[side, 2], lat=there),
            remote(count_v, near_count.at[side], dep_send.at[side, 3], dep_recv.at[side, 3], lat=there),
        ]

    def start_all(make):
        def action(side, there):
            for copy in make(side, there):
                copy.start()
        return action

    for side in (0, 1):
        with_neighbour(side, start_all(dep_sends))
    for c in range(min(AHEAD, CHUNKS)):
        for copy in raw_sends(c):
            copy.start()
    whole = pltpu.make_async_copy(conc, conc_v, local_sem.at[CHUNKS])
    whole.start()
    for c in range(CHUNKS):
        own_copy(c).start()

    def clear(side):
        def action():
            for c in range(CHUNKS):
                got[c][side] = jnp.zeros((ROWS, GROUP, LANES), jnp.bfloat16)
            for g in range(GROUPS):
                edges[g][side] = jnp.zeros((GROUP, WIDTH), jnp.bfloat16)
        pl.when(lat == (0 if side == 0 else n_lat - 1))(action)

    for side in (0, 1):
        clear(side)

    toep_v[...] = jnp.zeros_like(toep_v)
    toep_v[:, pl.ds(0, 2 * BINS - 1)] = toeplitz[...].astype(jnp.float32)
    for q in range(4):
        line = jnp.broadcast_to(toep_v[pl.ds(q, 1), :], (2 * BINS, 2 * BINS))
        turned = pltpu.roll(line, BINS + 1, 1, stride=1, stride_axis=0)
        taps[pl.ds(q * BINS, BINS), :] = turned.T[:BINS, :BINS].astype(jnp.bfloat16)
    diagonal = lax.broadcasted_iota(jnp.int32, (BINS, BINS), 0) == lax.broadcasted_iota(jnp.int32, (BINS, BINS), 1)
    sinking = jnp.sum(jnp.where(diagonal, jnp.broadcast_to(settle[...], (BINS, BINS)), 0.0), axis=1, keepdims=True)
    sinking = jnp.broadcast_to(sinking, (BINS, WIDTH))

    def fill(table, group, owner, row, weight, count):
        def one(r, _):
            number = jnp.int32(0)
            masses, total = [], jnp.float32(0.0)
            for k in range(ENTRIES):
                o = owner[k, r]
                mine = (o >= 5 * group) & (o < 5 * group + 5) & (k < count[0, r])
                w = jnp.where(mine, weight[k, r], jnp.float32(0.0))
                i = jnp.where(mine, (o - 5 * group) * ROWS + row[k, r], jnp.int32(2 * ROWS))
                number = number + jnp.where(mine, jnp.int32(1), jnp.int32(0))
                masses.append((w, mine))
                total = total + w
                index_s[table, r * ENTRIES + k] = i
            for k in range(ENTRIES):
                w, mine = masses[k]
                if table < 2:
                    w = jnp.where((number == 1) & mine, jnp.float32(1.0), w)
                mix_s[table, r * ENTRIES + k] = w
            return 0
        lax.fori_loop(0, ROWS, one, 0)

    def fill_scale(r, _):
        for side in (0, 1):
            group = 2 * side
            number, total = jnp.int32(0), jnp.float32(0.0)
            for k in range(ENTRIES):
                o = owner_s[k, r]
                mine = (o >= 5 * group) & (o < 5 * group + 5) & (k < count_s[0, r])
                number = number + jnp.where(mine, jnp.int32(1), jnp.int32(0))
                total = total + jnp.where(mine, weight_s[k, r], jnp.float32(0.0))
            scale_s[side, r] = jnp.where(number == 1, total, jnp.float32(1.0))
        return 0

    fill(2, 1, owner_s, row_s, weight_s, count_s)
    lax.fori_loop(0, ROWS, fill_scale, 0)

    def read_near(side, there):
        for copy in dep_arrivals(side, there):
            copy.wait_recv()
        moves = [
            pltpu.make_async_copy(near_int.at[side], near_int_s.at[side], own_int.at[side, 0]),
            pltpu.make_async_copy(near_weight.at[side], near_weight_s.at[side], own_int.at[side, 1]),
            pltpu.make_async_copy(near_count.at[side], near_count_s.at[side], own_int.at[side, 2]),
        ]
        for move in moves:
            move.start()
        for move in moves:
            move.wait()
        fill(side, 2 - 2 * side, near_int_s.at[side, 0], near_int_s.at[side, 1], near_weight_s.at[side],
             near_count_s.at[side])

    for side in (0, 1):
        with_neighbour(side, read_near)

    whole.wait()

    def grow(r, _):
        cells = conc_v[r]
        product = jnp.dot(taps[...], cells, preferred_element_type=jnp.float32)
        total = -sinking * cells.astype(jnp.float32)
        for q in range(4):
            total = total + rates[q, pl.ds(r, 1), :] * product[q * BINS:(q + 1) * BINS]
        base[r] = total
        return 0

    lax.fori_loop(0, ROWS, grow, 0)

    def mixed(c, table, r):
        total = jnp.zeros((GROUP, LANES), jnp.float32)
        for k in range(ENTRIES):
            place = index_s[table, r * ENTRIES + k]
            total = total + mix_s[table, r * ENTRIES + k] * held[c][place].astype(jnp.float32)
        return total

    def part_send_copy(c, side, there):
        return remote(
            sent[c].at[side], got[c].at[1 - side], part_send.at[c, side], part_recv.at[c, 1 - side], lat=there
        )

    def part_arrival(c, side, there):
        return remote(
            sent[c].at[side], got[c].at[side], part_send.at[c, side], part_recv.at[c, side], lat=there
        )

    def partials(c):
        def action(side, there):
            def one(r, _):
                sent[c][side, r] = mixed(c, side, r).astype(jnp.bfloat16)
                return 0
            lax.fori_loop(0, ROWS, one, 0, unroll=2)
            part_send_copy(c, side, there).start()
        for side in (0, 1):
            with_neighbour(side, action)

    def remap(c):
        g, h = c // HALVES, c % HALVES
        for side in (0, 1):
            with_neighbour(side, lambda side, there: part_arrival(c, side, there).wait_recv())

        def one(r, _):
            total = mixed(c, 2, r)
            for side in (0, 1):
                total = total + scale_s[side, r] * got[c][side, r].astype(jnp.float32)
            remapped[g][r, :, pl.ds(h * LANES, LANES)] = total.astype(jnp.bfloat16)
            return 0

        lax.fori_loop(0, ROWS, one, 0, unroll=2)

    def strip_sends(g):
        return [
            remote(remapped[g].at[:, :, pl.ds(0, STRIP)], strips[g].at[1],
                   strip_send.at[g, 0], strip_recv.at[g, 1], lon=west),
            remote(remapped[g].at[:, :, pl.ds(WIDTH - STRIP, STRIP)], strips[g].at[0],
                   strip_send.at[g, 1], strip_recv.at[g, 0], lon=east),
        ]

    def strip_arrivals(g):
        return [
            remote(remapped[g].at[:, :, pl.ds(0, STRIP)], strips[g].at[side],
                   strip_send.at[g, side], strip_recv.at[g, side], lon=west)
            for side in (0, 1)
        ]

    span = WIDTH + 2 * STRIP

    def shifted(g, r):
        line = jnp.concatenate([strips[g][0, r], remapped[g][r], strips[g][1, r]], axis=1).astype(jnp.float32)
        step = offset_s[r]
        line = pltpu.roll(line, jnp.where(step < 0, step + span, step), 1)
        beside = pltpu.roll(line, 1, 1) + pltpu.roll(line, span - 1, 1)
        return line[:, STRIP:STRIP + WIDTH], beside[:, STRIP:STRIP + WIDTH]

    def edge_copy(g, side, there):
        return remote(
            ends[g].at[side], edges[g].at[1 - side], edge_send.at[g, side], edge_recv.at[g, 1 - side], lat=there
        )

    def edge_arrival(g, side, there):
        return remote(
            ends[g].at[side], edges[g].at[side], edge_send.at[g, side], edge_recv.at[g, side], lat=there
        )

    def outer_rows(g):
        for copy in strip_arrivals(g):
            copy.wait_recv()

        def action(side, there):
            center, _ = shifted(g, 0 if side == 0 else ROWS - 1)
            ends[g][side] = center.astype(jnp.bfloat16)
            edge_copy(g, side, there).start()

        for side in (0, 1):
            with_neighbour(side, action)

    def out_copy(g):
        return pltpu.make_async_copy(
            base.at[:, pl.ds(g * GROUP, GROUP), :], out.at[:, pl.ds(g * GROUP, GROUP), :], out_sem.at[g]
        )

    def finish(g):
        for side in (0, 1):
            with_neighbour(side, lambda side, there: edge_arrival(g, side, there).wait_recv())

        def emit(r, above, center, beside, below):
            total = base[r, pl.ds(g * GROUP, GROUP), :] + center
            base[r, pl.ds(g * GROUP, GROUP), :] = total + kappa[pl.ds(r, 1), :] * (
                (above + below) + beside - 4.0 * center
            )

        def one(r, carry):
            above, center, beside = carry
            below, below_beside = shifted(g, r + 1)
            emit(r, above, center, beside, below)
            return center, below, below_beside

        center, beside = shifted(g, 0)
        above = edges[g][0].astype(jnp.float32)
        above, center, beside = lax.fori_loop(0, ROWS - 1, one, (above, center, beside))
        emit(ROWS - 1, above, center, beside, edges[g][1].astype(jnp.float32))
        out_copy(g).start()

    for c in range(CHUNKS):
        for which in (0, 1):
            raw_arrival(c, which).wait_recv()
        forward(c).start()
        if c + AHEAD < CHUNKS:
            for copy in raw_sends(c + AHEAD):
                copy.start()
        own_copy(c).wait()
        for which in (2, 3):
            raw_arrival(c, which).wait_recv()
        partials(c)
        if c >= 1:
            remap(c - 1)
            if (c - 1) % HALVES == HALVES - 1:
                for copy in strip_sends((c - 1) // HALVES):
                    copy.start()
        if c % HALVES == 0 and c // HALVES >= 2:
            outer_rows(c // HALVES - 2)
        if c % HALVES == 0 and c // HALVES >= 3:
            finish(c // HALVES - 3)
    if GROUPS >= 3:
        finish(GROUPS - 3)
    outer_rows(GROUPS - 2)
    remap(CHUNKS - 1)
    for copy in strip_sends(GROUPS - 1):
        copy.start()
    finish(GROUPS - 2)
    outer_rows(GROUPS - 1)
    finish(GROUPS - 1)

    for c in range(CHUNKS):
        for copy in raw_sends(c):
            copy.wait_send()
        forward(c).wait_send()
        for side in (0, 1):
            with_neighbour(side, lambda side, there: part_send_copy(c, side, there).wait_send())
    for g in range(GROUPS):
        for copy in strip_sends(g):
            copy.wait_send()
        for side in (0, 1):
            with_neighbour(side, lambda side, there: edge_copy(g, side, there).wait_send())
        out_copy(g).wait()

    def dep_sent(side, there):
        for copy in dep_sends(side, there):
            copy.wait_send()

    for side in (0, 1):
        with_neighbour(side, dep_sent)


def solution(mesh):
    n_lat, n_lon = mesh.shape["lat"], mesh.shape["lon"]

    def body(conc, dep_owner, dep_row, dep_weight, dep_count, zonal_offset, agg_rates, toeplitz, settle, kappa):
        owner, row, weight = dep_owner[0].T, dep_row[0].T, dep_weight[0].T
        any_space = pl.BlockSpec(memory_space=pl.ANY)
        vmem = pl.BlockSpec(memory_space=pltpu.VMEM)
        smem = pl.BlockSpec(memory_space=pltpu.SMEM)
        bf16, f32, i32 = jnp.bfloat16, jnp.float32, jnp.int32
        dma = pltpu.SemaphoreType.DMA
        return pl.pallas_call(
            functools.partial(kernel, n_lat, n_lon),
            out_shape=jax.ShapeDtypeStruct((ROWS, BINS, WIDTH), f32),
            in_specs=[any_space, vmem, vmem, vmem, vmem, smem, smem, smem, smem, smem, vmem, vmem, vmem, vmem],
            out_specs=any_space,
            scratch_shapes=[
                pltpu.VMEM((ROWS, BINS, WIDTH), bf16),
                pltpu.VMEM((ROWS, BINS, WIDTH), f32),
                pltpu.VMEM((4 * BINS, BINS), bf16),
                pltpu.VMEM((4, 2 * BINS), f32),
                pltpu.VMEM((2, 2, ENTRIES, ROWS), i32),
                pltpu.VMEM((2, ENTRIES, ROWS), f32),
                pltpu.VMEM((2, 1, ROWS), i32),
                dma((2, 3)),
                pltpu.SMEM((2, 2, ENTRIES, ROWS), i32),
                pltpu.SMEM((2, ENTRIES, ROWS), f32),
                pltpu.SMEM((2, 1, ROWS), i32),
                pltpu.SMEM((3, ROWS * ENTRIES), i32),
                pltpu.SMEM((3, ROWS * ENTRIES), f32),
                pltpu.SMEM((2, ROWS), f32),
            ]
            + [pltpu.VMEM((5 * ROWS, GROUP, LANES), bf16) for _ in range(CHUNKS)]
            + [pltpu.VMEM((2, ROWS, GROUP, LANES), bf16) for _ in range(2 * CHUNKS)]
            + [pltpu.VMEM((ROWS, GROUP, WIDTH), bf16) for _ in range(GROUPS)]
            + [pltpu.VMEM((2, ROWS, GROUP, STRIP), bf16) for _ in range(GROUPS)]
            + [pltpu.VMEM((2, GROUP, WIDTH), bf16) for _ in range(2 * GROUPS)]
            + [
                dma((2, 4)), dma((2, 4)),
                dma((CHUNKS, 4)), dma((CHUNKS, 4)),
                dma((CHUNKS, 2)), dma((CHUNKS, 2)),
                dma((GROUPS, 2)), dma((GROUPS, 2)),
                dma((GROUPS, 2)), dma((GROUPS, 2)),
                dma((CHUNKS + 1,)), dma((GROUPS,)),
            ],
            compiler_params=pltpu.CompilerParams(
                collective_id=0, has_side_effects=True, vmem_limit_bytes=40 << 20
            ),
            name="remap_step",
        )(
            conc, owner, row, weight, dep_count, owner, row, weight, dep_count, zonal_offset,
            agg_rates, toeplitz, settle.reshape(1, BINS), kappa,
        )

    return jax.shard_map(
        body,
        mesh=mesh,
        in_specs=(
            P("lat", None, "lon"),
            P("lon", "lat", None),
            P("lon", "lat", None),
            P("lon", "lat", None),
            P("lon", "lat"),
            P("lat"),
            P(None, "lat", "lon"),
            P(),
            P(),
            P("lat", "lon"),
        ),
        out_specs=P("lat", None, "lon"),
        check_vma=False,
    )
```

```python
import functools

import jax
import jax.numpy as jnp
from jax import lax
from jax.experimental import pallas as pl
from jax.experimental.pallas import tpu as pltpu
from jax.sharding import PartitionSpec as P

MESH = pl.DeviceIdType.MESH
ROWS = 32
BINS = 64
WIDTH = 256
ENTRIES = 4
GROUP = 16
GROUPS = BINS // GROUP
HALVES = 1
LANES = WIDTH // HALVES
CHUNKS = GROUPS * HALVES
AHEAD = 2
STRIP = 128


def kernel(
    n_lat, n_lon,
    conc, owner_h, row_h, weight_h, count_h, offset_h, rates_h, toeplitz_h, settle_h, kappa_h,
    base,
    owner_s, row_s, weight_s, count_s, offset_s, rates, toeplitz, settle, kappa,
    conc_v, taps, toep_v, near_int, near_weight, near_count,
    fetch_sem, own_int, near_int_s, near_weight_s, near_count_s, index_s, mix_s, scale_s,
    *rest,
):
    held = rest[0:CHUNKS]
    sent = rest[CHUNKS:2 * CHUNKS]
    got = rest[2 * CHUNKS:3 * CHUNKS]
    remapped = rest[3 * CHUNKS:3 * CHUNKS + GROUPS]
    strips = rest[3 * CHUNKS + GROUPS:3 * CHUNKS + 2 * GROUPS]
    ends = rest[3 * CHUNKS + 2 * GROUPS:3 * CHUNKS + 3 * GROUPS]
    edges = rest[3 * CHUNKS + 3 * GROUPS:3 * CHUNKS + 4 * GROUPS]
    (dep_send, dep_recv, raw_send, raw_recv, part_send, part_recv,
     strip_send, strip_recv, edge_send, edge_recv, local_sem) = rest[3 * CHUNKS + 4 * GROUPS:]

    lat = lax.axis_index("lat")
    lon = lax.axis_index("lon")
    core = lax.rem(lon, 2)
    chip = lon - core

    def at_lon(value):
        return lax.rem(value + 2 * n_lon, n_lon)

    sibling = chip + 1 - core
    after = at_lon(chip + 2)
    before = at_lon(chip - 1)
    west, east = at_lon(lon - 1), at_lon(lon + 1)

    fetches = [
        pltpu.make_async_copy(src, dst, fetch_sem.at[i])
        for i, (src, dst) in enumerate([
            (owner_h, owner_s), (row_h, row_s), (weight_h, weight_s), (count_h, count_s), (offset_h, offset_s),
            (toeplitz_h, toeplitz), (settle_h, settle), (rates_h, rates), (kappa_h, kappa), (conc, conc_v),
        ])
    ]
    for fetch in fetches:
        fetch.start()

    barrier = pltpu.get_barrier_semaphore()
    for step in (-2, -1, 1, 2):
        pl.semaphore_signal(barrier, inc=1, device_id={"lon": at_lon(lon + step)}, device_id_type=MESH)

    def with_neighbour(side, action):
        inside = lat > 0 if side == 0 else lat < n_lat - 1
        pl.when(inside)(functools.partial(action, side, lat - 1 if side == 0 else lat + 1))

    def greet(side, there):
        pl.semaphore_signal(barrier, inc=1, device_id={"lat": there}, device_id_type=MESH)

    for side in (0, 1):
        with_neighbour(side, greet)
    pl.semaphore_wait(barrier, 4 + jnp.where(lat > 0, 1, 0) + jnp.where(lat < n_lat - 1, 1, 0))

    def remote(src, dst, send, recv, **where):
        return pltpu.make_async_remote_copy(
            src_ref=src, dst_ref=dst, send_sem=send, recv_sem=recv, device_id=where, device_id_type=MESH
        )

    def window(c):
        g, h = c // HALVES, c % HALVES
        return conc.at[:, pl.ds(g * GROUP, GROUP), pl.ds(h * LANES, LANES)]

    def slot(c, number):
        return held[c].at[pl.ds(number * ROWS, ROWS)]

    def raw_sends(c):
        return [
            remote(window(c), slot(c, core), raw_send.at[c, 0], raw_recv.at[c, core], lon=after),
            remote(window(c), slot(c, core + 3), raw_send.at[c, 1], raw_recv.at[c, core], lon=before),
            remote(window(c), slot(c, 1 + 2 * core), raw_send.at[c, 2], raw_recv.at[c, 2], lon=sibling),
        ]

    far = 3 * core

    def raw_arrival(c, which):
        number = (far, far + 1, 3 - 2 * core, 4 - 4 * core)[which]
        return remote(window(c), slot(c, number), raw_send.at[c, 3], raw_recv.at[c, which], lon=sibling)

    def forward(c):
        return remote(
            slot(c, 1 + 2 * core), slot(c, 4 * core), raw_send.at[c, 3], raw_recv.at[c, 3], lon=sibling
        )

    def own_copy(c):
        return pltpu.make_async_copy(window(c), slot(c, 2), local_sem.at[c])

    def dep_sends(side, there):
        other = 1 - side
        return [
            remote(owner_h, near_int.at[other, 0], dep_send.at[side, 0], dep_recv.at[other, 0], lat=there),
            remote(row_h, near_int.at[other, 1], dep_send.at[side, 1], dep_recv.at[other, 1], lat=there),
            remote(weight_h, near_weight.at[other], dep_send.at[side, 2], dep_recv.at[other, 2], lat=there),
            remote(count_h, near_count.at[other], dep_send.at[side, 3], dep_recv.at[other, 3], lat=there),
        ]

    def dep_arrivals(side, there):
        return [
            remote(owner_h, near_int.at[side, 0], dep_send.at[side, 0], dep_recv.at[side, 0], lat=there),
            remote(row_h, near_int.at[side, 1], dep_send.at[side, 1], dep_recv.at[side, 1], lat=there),
            remote(weight_h, near_weight.at[side], dep_send.at[side, 2], dep_recv.at[side, 2], lat=there),
            remote(count_h, near_count.at[side], dep_send.at[side, 3], dep_recv.at[side, 3], lat=there),
        ]

    def start_all(make):
        def action(side, there):
            for copy in make(side, there):
                copy.start()
        return action

    for side in (0, 1):
        with_neighbour(side, start_all(dep_sends))
    for c in range(min(AHEAD, CHUNKS)):
        for copy in raw_sends(c):
            copy.start()
    for c in range(CHUNKS):
        own_copy(c).start()

    def clear(side):
        def action():
            for c in range(CHUNKS):
                got[c][side] = jnp.zeros((ROWS, GROUP, LANES), jnp.bfloat16)
            for g in range(GROUPS):
                edges[g][side] = jnp.zeros((GROUP, WIDTH), jnp.bfloat16)
        pl.when(lat == (0 if side == 0 else n_lat - 1))(action)

    for side in (0, 1):
        clear(side)

    for fetch in fetches[5:7]:
        fetch.wait()

    toep_v[...] = jnp.zeros_like(toep_v)
    toep_v[:, pl.ds(0, 2 * BINS - 1)] = toeplitz[...].astype(jnp.float32)
    for q in range(4):
        line = jnp.broadcast_to(toep_v[pl.ds(q, 1), :], (2 * BINS, 2 * BINS))
        turned = pltpu.roll(line, BINS + 1, 1, stride=1, stride_axis=0)
        taps[pl.ds(q * BINS, BINS), :] = turned.T[:BINS, :BINS].astype(jnp.bfloat16)
    diagonal = lax.broadcasted_iota(jnp.int32, (BINS, BINS), 0) == lax.broadcasted_iota(jnp.int32, (BINS, BINS), 1)
    sinking = jnp.sum(jnp.where(diagonal, jnp.broadcast_to(settle[...], (BINS, BINS)), 0.0), axis=1, keepdims=True)
    sinking = jnp.broadcast_to(sinking, (BINS, WIDTH))

    def fill(table, group, owner, row, weight, count):
        def one(r, _):
            number = jnp.int32(0)
            masses, total = [], jnp.float32(0.0)
            for k in range(ENTRIES):
                o = owner[k, r]
                mine = (o >= 5 * group) & (o < 5 * group + 5) & (k < count[0, r])
                w = jnp.where(mine, weight[k, r], jnp.float32(0.0))
                i = jnp.where(mine, (o - 5 * group) * ROWS + row[k, r], jnp.int32(2 * ROWS))
                number = number + jnp.where(mine, jnp.int32(1), jnp.int32(0))
                masses.append((w, mine))
                total = total + w
                index_s[table, r * ENTRIES + k] = i
            for k in range(ENTRIES):
                w, mine = masses[k]
                if table < 2:
                    w = jnp.where((number == 1) & mine, jnp.float32(1.0), w)
                mix_s[table, r * ENTRIES + k] = w
            return 0
        lax.fori_loop(0, ROWS, one, 0)

    def fill_scale(r, _):
        for side in (0, 1):
            group = 2 * side
            number, total = jnp.int32(0), jnp.float32(0.0)
            for k in range(ENTRIES):
                o = owner_s[k, r]
                mine = (o >= 5 * group) & (o < 5 * group + 5) & (k < count_s[0, r])
                number = number + jnp.where(mine, jnp.int32(1), jnp.int32(0))
                total = total + jnp.where(mine, weight_s[k, r], jnp.float32(0.0))
            scale_s[side, r] = jnp.where(number == 1, total, jnp.float32(1.0))
        return 0

    for fetch in fetches[:5]:
        fetch.wait()
    fill(2, 1, owner_s, row_s, weight_s, count_s)
    lax.fori_loop(0, ROWS, fill_scale, 0)

    def read_near(side, there):
        for copy in dep_arrivals(side, there):
            copy.wait_recv()
        moves = [
            pltpu.make_async_copy(near_int.at[side], near_int_s.at[side], own_int.at[side, 0]),
            pltpu.make_async_copy(near_weight.at[side], near_weight_s.at[side], own_int.at[side, 1]),
            pltpu.make_async_copy(near_count.at[side], near_count_s.at[side], own_int.at[side, 2]),
        ]
        for move in moves:
            move.start()
        for move in moves:
            move.wait()
        fill(side, 2 - 2 * side, near_int_s.at[side, 0], near_int_s.at[side, 1], near_weight_s.at[side],
             near_count_s.at[side])

    for side in (0, 1):
        with_neighbour(side, read_near)

    for fetch in fetches[7:]:
        fetch.wait()

    def grow(r, _):
        cells = conc_v[r]
        product = jnp.dot(taps[...], cells, preferred_element_type=jnp.float32)
        total = -sinking * cells.astype(jnp.float32)
        for q in range(4):
            total = total + rates[q, pl.ds(r, 1), :] * product[q * BINS:(q + 1) * BINS]
        base[r] = total
        return 0

    lax.fori_loop(0, ROWS, grow, 0)

    def mixed(c, table, r):
        total = jnp.zeros((GROUP, LANES), jnp.float32)
        for k in range(ENTRIES):
            place = index_s[table, r * ENTRIES + k]
            total = total + mix_s[table, r * ENTRIES + k] * held[c][place].astype(jnp.float32)
        return total

    def part_send_copy(c, side, there):
        return remote(
            sent[c].at[side], got[c].at[1 - side], part_send.at[c, side], part_recv.at[c, 1 - side], lat=there
        )

    def part_arrival(c, side, there):
        return remote(
            sent[c].at[side], got[c].at[side], part_send.at[c, side], part_recv.at[c, side], lat=there
        )

    def partials(c):
        def action(side, there):
            def one(r, _):
                sent[c][side, r] = mixed(c, side, r).astype(jnp.bfloat16)
                return 0
            lax.fori_loop(0, ROWS, one, 0, unroll=2)
            part_send_copy(c, side, there).start()
        for side in (0, 1):
            with_neighbour(side, action)

    def remap(c):
        g, h = c // HALVES, c % HALVES
        for side in (0, 1):
            with_neighbour(side, lambda side, there: part_arrival(c, side, there).wait_recv())

        def one(r, _):
            total = mixed(c, 2, r)
            for side in (0, 1):
                total = total + scale_s[side, r] * got[c][side, r].astype(jnp.float32)
            remapped[g][r, :, pl.ds(h * LANES, LANES)] = total.astype(jnp.bfloat16)
            return 0

        lax.fori_loop(0, ROWS, one, 0, unroll=2)

    def strip_sends(g):
        return [
            remote(remapped[g].at[:, :, pl.ds(0, STRIP)], strips[g].at[1],
                   strip_send.at[g, 0], strip_recv.at[g, 1], lon=west),
            remote(remapped[g].at[:, :, pl.ds(WIDTH - STRIP, STRIP)], strips[g].at[0],
                   strip_send.at[g, 1], strip_recv.at[g, 0], lon=east),
        ]

    def strip_arrivals(g):
        return [
            remote(remapped[g].at[:, :, pl.ds(0, STRIP)], strips[g].at[side],
                   strip_send.at[g, side], strip_recv.at[g, side], lon=west)
            for side in (0, 1)
        ]

    span = WIDTH + 2 * STRIP

    def shifted(g, r):
        line = jnp.concatenate([strips[g][0, r], remapped[g][r], strips[g][1, r]], axis=1).astype(jnp.float32)
        step = offset_s[r]
        line = pltpu.roll(line, jnp.where(step < 0, step + span, step), 1)
        beside = pltpu.roll(line, 1, 1) + pltpu.roll(line, span - 1, 1)
        return line[:, STRIP:STRIP + WIDTH], beside[:, STRIP:STRIP + WIDTH]

    def edge_copy(g, side, there):
        return remote(
            ends[g].at[side], edges[g].at[1 - side], edge_send.at[g, side], edge_recv.at[g, 1 - side], lat=there
        )

    def edge_arrival(g, side, there):
        return remote(
            ends[g].at[side], edges[g].at[side], edge_send.at[g, side], edge_recv.at[g, side], lat=there
        )

    def outer_rows(g):
        for copy in strip_arrivals(g):
            copy.wait_recv()

        def action(side, there):
            center, _ = shifted(g, 0 if side == 0 else ROWS - 1)
            ends[g][side] = center.astype(jnp.bfloat16)
            edge_copy(g, side, there).start()

        for side in (0, 1):
            with_neighbour(side, action)

    def finish(g):
        for side in (0, 1):
            with_neighbour(side, lambda side, there: edge_arrival(g, side, there).wait_recv())

        def emit(r, above, center, beside, below):
            total = base[r, pl.ds(g * GROUP, GROUP), :] + center
            base[r, pl.ds(g * GROUP, GROUP), :] = total + kappa[pl.ds(r, 1), :] * (
                (above + below) + beside - 4.0 * center
            )

        def one(r, carry):
            above, center, beside = carry
            below, below_beside = shifted(g, r + 1)
            emit(r, above, center, beside, below)
            return center, below, below_beside

        center, beside = shifted(g, 0)
        above = edges[g][0].astype(jnp.float32)
        above, center, beside = lax.fori_loop(0, ROWS - 1, one, (above, center, beside))
        emit(ROWS - 1, above, center, beside, edges[g][1].astype(jnp.float32))

    for c in range(CHUNKS):
        for which in (0, 1):
            raw_arrival(c, which).wait_recv()
        forward(c).start()
        if c + AHEAD < CHUNKS:
            for copy in raw_sends(c + AHEAD):
                copy.start()
        own_copy(c).wait()
        for which in (2, 3):
            raw_arrival(c, which).wait_recv()
        partials(c)
        if c >= 1:
            remap(c - 1)
            if (c - 1) % HALVES == HALVES - 1:
                for copy in strip_sends((c - 1) // HALVES):
                    copy.start()
        if c % HALVES == 0 and c // HALVES >= 2:
            outer_rows(c // HALVES - 2)
        if c % HALVES == 0 and c // HALVES >= 3:
            finish(c // HALVES - 3)
    if GROUPS >= 3:
        finish(GROUPS - 3)
    outer_rows(GROUPS - 2)
    remap(CHUNKS - 1)
    for copy in strip_sends(GROUPS - 1):
        copy.start()
    finish(GROUPS - 2)
    outer_rows(GROUPS - 1)
    finish(GROUPS - 1)

    for c in range(CHUNKS):
        for copy in raw_sends(c):
            copy.wait_send()
        forward(c).wait_send()
        for side in (0, 1):
            with_neighbour(side, lambda side, there: part_send_copy(c, side, there).wait_send())
    for g in range(GROUPS):
        for copy in strip_sends(g):
            copy.wait_send()
        for side in (0, 1):
            with_neighbour(side, lambda side, there: edge_copy(g, side, there).wait_send())

    def dep_sent(side, there):
        for copy in dep_sends(side, there):
            copy.wait_send()

    for side in (0, 1):
        with_neighbour(side, dep_sent)


def solution(mesh):
    n_lat, n_lon = mesh.shape["lat"], mesh.shape["lon"]

    def body(conc, dep_owner, dep_row, dep_weight, dep_count, zonal_offset, agg_rates, toeplitz, settle, kappa):
        owner, row, weight = dep_owner[0].T, dep_row[0].T, dep_weight[0].T
        hbm = pl.BlockSpec(memory_space=pltpu.HBM)
        bf16, f32, i32 = jnp.bfloat16, jnp.float32, jnp.int32
        dma = pltpu.SemaphoreType.DMA
        return pl.pallas_call(
            functools.partial(kernel, n_lat, n_lon),
            out_shape=jax.ShapeDtypeStruct((ROWS, BINS, WIDTH), f32),
            in_specs=[hbm] * 10,
            out_specs=pl.BlockSpec(memory_space=pltpu.VMEM),
            scratch_shapes=[
                pltpu.SMEM((ENTRIES, ROWS), i32),
                pltpu.SMEM((ENTRIES, ROWS), i32),
                pltpu.SMEM((ENTRIES, ROWS), f32),
                pltpu.SMEM((1, ROWS), i32),
                pltpu.SMEM((ROWS,), i32),
                pltpu.VMEM((4, ROWS, WIDTH), f32),
                pltpu.VMEM((4, 2 * BINS - 1), bf16),
                pltpu.VMEM((1, BINS), f32),
                pltpu.VMEM((ROWS, WIDTH), f32),
                pltpu.VMEM((ROWS, BINS, WIDTH), bf16),
                pltpu.VMEM((4 * BINS, BINS), bf16),
                pltpu.VMEM((4, 2 * BINS), f32),
                pltpu.VMEM((2, 2, ENTRIES, ROWS), i32),
                pltpu.VMEM((2, ENTRIES, ROWS), f32),
                pltpu.VMEM((2, 1, ROWS), i32),
                dma((10,)),
                dma((2, 3)),
                pltpu.SMEM((2, 2, ENTRIES, ROWS), i32),
                pltpu.SMEM((2, ENTRIES, ROWS), f32),
                pltpu.SMEM((2, 1, ROWS), i32),
                pltpu.SMEM((3, ROWS * ENTRIES), i32),
                pltpu.SMEM((3, ROWS * ENTRIES), f32),
                pltpu.SMEM((2, ROWS), f32),
            ]
            + [pltpu.VMEM((5 * ROWS, GROUP, LANES), bf16) for _ in range(CHUNKS)]
            + [pltpu.VMEM((2, ROWS, GROUP, LANES), bf16) for _ in range(2 * CHUNKS)]
            + [pltpu.VMEM((ROWS, GROUP, WIDTH), bf16) for _ in range(GROUPS)]
            + [pltpu.VMEM((2, ROWS, GROUP, STRIP), bf16) for _ in range(GROUPS)]
            + [pltpu.VMEM((2, GROUP, WIDTH), bf16) for _ in range(2 * GROUPS)]
            + [
                dma((2, 4)), dma((2, 4)),
                dma((CHUNKS, 4)), dma((CHUNKS, 4)),
                dma((CHUNKS, 2)), dma((CHUNKS, 2)),
                dma((GROUPS, 2)), dma((GROUPS, 2)),
                dma((GROUPS, 2)), dma((GROUPS, 2)),
                dma((CHUNKS,)),
            ],
            compiler_params=pltpu.CompilerParams(
                collective_id=0, has_side_effects=True, vmem_limit_bytes=40 << 20
            ),
            name="remap_step",
        )(
            *[
                pltpu.with_memory_space_constraint(operand, pltpu.HBM)
                for operand in (
                    conc, owner, row, weight, dep_count, zonal_offset, agg_rates, toeplitz,
                    settle.reshape(1, BINS), kappa,
                )
            ]
        )

    return jax.shard_map(
        body,
        mesh=mesh,
        in_specs=(
            P("lat", None, "lon"),
            P("lon", "lat", None),
            P("lon", "lat", None),
            P("lon", "lat", None),
            P("lon", "lat"),
            P("lat"),
            P(None, "lat", "lon"),
            P(),
            P(),
            P("lat", "lon"),
        ),
        out_specs=P("lat", None, "lon"),
        check_vma=False,
    )
```

```python
import functools

import jax
import jax.numpy as jnp
from jax import lax
from jax.experimental import pallas as pl
from jax.experimental.pallas import tpu as pltpu
from jax.sharding import PartitionSpec as P

MESH = pl.DeviceIdType.MESH
ROWS = 32
BINS = 64
WIDTH = 256
ENTRIES = 4
GROUP = 16
GROUPS = BINS // GROUP
HALVES = 1
LANES = WIDTH // HALVES
CHUNKS = GROUPS * HALVES
AHEAD = 2
STRIP = 128


def kernel(
    n_lat, n_lon,
    conc, owner_h, row_h, weight_h, count_h, offset_h, rates_h, toeplitz_h, settle_h, kappa_h,
    base,
    owner_s, row_s, weight_s, count_s, offset_s, rates, toeplitz, settle, kappa,
    conc_v, taps, toep_v, near_int, near_weight, near_count,
    fetch_sem, own_int, near_int_s, near_weight_s, near_count_s, index_s, mix_s, scale_s,
    *rest,
):
    held = rest[0:CHUNKS]
    sent = rest[CHUNKS:2 * CHUNKS]
    got = rest[2 * CHUNKS:3 * CHUNKS]
    remapped = rest[3 * CHUNKS:3 * CHUNKS + GROUPS]
    strips = rest[3 * CHUNKS + GROUPS:3 * CHUNKS + 2 * GROUPS]
    ends = rest[3 * CHUNKS + 2 * GROUPS:3 * CHUNKS + 3 * GROUPS]
    edges = rest[3 * CHUNKS + 3 * GROUPS:3 * CHUNKS + 4 * GROUPS]
    centers = rest[3 * CHUNKS + 4 * GROUPS:3 * CHUNKS + 5 * GROUPS]
    besides = rest[3 * CHUNKS + 5 * GROUPS:3 * CHUNKS + 6 * GROUPS]
    (dep_send, dep_recv, raw_send, raw_recv, part_send, part_recv,
     strip_send, strip_recv, edge_send, edge_recv, local_sem) = rest[3 * CHUNKS + 6 * GROUPS:]

    lat = lax.axis_index("lat")
    lon = lax.axis_index("lon")
    core = lax.rem(lon, 2)
    chip = lon - core

    def at_lon(value):
        return lax.rem(value + 2 * n_lon, n_lon)

    sibling = chip + 1 - core
    after = at_lon(chip + 2)
    before = at_lon(chip - 1)
    west, east = at_lon(lon - 1), at_lon(lon + 1)

    fetches = [
        pltpu.make_async_copy(src, dst, fetch_sem.at[i])
        for i, (src, dst) in enumerate([
            (owner_h, owner_s), (row_h, row_s), (weight_h, weight_s), (count_h, count_s), (offset_h, offset_s),
            (toeplitz_h, toeplitz), (settle_h, settle), (rates_h, rates), (kappa_h, kappa), (conc, conc_v),
        ])
    ]
    for fetch in fetches:
        fetch.start()

    barrier = pltpu.get_barrier_semaphore()
    for step in (-2, -1, 1, 2):
        pl.semaphore_signal(barrier, inc=1, device_id={"lon": at_lon(lon + step)}, device_id_type=MESH)

    def with_neighbour(side, action):
        inside = lat > 0 if side == 0 else lat < n_lat - 1
        pl.when(inside)(functools.partial(action, side, lat - 1 if side == 0 else lat + 1))

    def greet(side, there):
        pl.semaphore_signal(barrier, inc=1, device_id={"lat": there}, device_id_type=MESH)

    for side in (0, 1):
        with_neighbour(side, greet)
    pl.semaphore_wait(barrier, 4 + jnp.where(lat > 0, 1, 0) + jnp.where(lat < n_lat - 1, 1, 0))

    def remote(src, dst, send, recv, **where):
        return pltpu.make_async_remote_copy(
            src_ref=src, dst_ref=dst, send_sem=send, recv_sem=recv, device_id=where, device_id_type=MESH
        )

    def window(c):
        g, h = c // HALVES, c % HALVES
        return conc.at[:, pl.ds(g * GROUP, GROUP), pl.ds(h * LANES, LANES)]

    def slot(c, number):
        return held[c].at[pl.ds(number * ROWS, ROWS)]

    def raw_sends(c):
        return [
            remote(window(c), slot(c, core), raw_send.at[c, 0], raw_recv.at[c, core], lon=after),
            remote(window(c), slot(c, core + 3), raw_send.at[c, 1], raw_recv.at[c, core], lon=before),
            remote(window(c), slot(c, 1 + 2 * core), raw_send.at[c, 2], raw_recv.at[c, 2], lon=sibling),
        ]

    far = 3 * core

    def raw_arrival(c, which):
        number = (far, far + 1, 3 - 2 * core, 4 - 4 * core)[which]
        return remote(window(c), slot(c, number), raw_send.at[c, 3], raw_recv.at[c, which], lon=sibling)

    def forward(c):
        return remote(
            slot(c, 1 + 2 * core), slot(c, 4 * core), raw_send.at[c, 3], raw_recv.at[c, 3], lon=sibling
        )

    def own_copy(c):
        return pltpu.make_async_copy(window(c), slot(c, 2), local_sem.at[c])

    def dep_sends(side, there):
        other = 1 - side
        return [
            remote(owner_h, near_int.at[other, 0], dep_send.at[side, 0], dep_recv.at[other, 0], lat=there),
            remote(row_h, near_int.at[other, 1], dep_send.at[side, 1], dep_recv.at[other, 1], lat=there),
            remote(weight_h, near_weight.at[other], dep_send.at[side, 2], dep_recv.at[other, 2], lat=there),
            remote(count_h, near_count.at[other], dep_send.at[side, 3], dep_recv.at[other, 3], lat=there),
        ]

    def dep_arrivals(side, there):
        return [
            remote(owner_h, near_int.at[side, 0], dep_send.at[side, 0], dep_recv.at[side, 0], lat=there),
            remote(row_h, near_int.at[side, 1], dep_send.at[side, 1], dep_recv.at[side, 1], lat=there),
            remote(weight_h, near_weight.at[side], dep_send.at[side, 2], dep_recv.at[side, 2], lat=there),
            remote(count_h, near_count.at[side], dep_send.at[side, 3], dep_recv.at[side, 3], lat=there),
        ]

    def start_all(make):
        def action(side, there):
            for copy in make(side, there):
                copy.start()
        return action

    for side in (0, 1):
        with_neighbour(side, start_all(dep_sends))
    for c in range(min(AHEAD, CHUNKS)):
        for copy in raw_sends(c):
            copy.start()
    for c in range(CHUNKS):
        own_copy(c).start()

    def clear(side):
        def action():
            for c in range(CHUNKS):
                got[c][side] = jnp.zeros((ROWS, GROUP, LANES), jnp.bfloat16)
            for g in range(GROUPS):
                edges[g][side] = jnp.zeros((GROUP, WIDTH), jnp.bfloat16)
        pl.when(lat == (0 if side == 0 else n_lat - 1))(action)

    for side in (0, 1):
        clear(side)

    for fetch in fetches[5:7]:
        fetch.wait()

    toep_v[...] = jnp.zeros_like(toep_v)
    toep_v[:, pl.ds(0, 2 * BINS - 1)] = toeplitz[...].astype(jnp.float32)
    for q in range(4):
        line = jnp.broadcast_to(toep_v[pl.ds(q, 1), :], (2 * BINS, 2 * BINS))
        turned = pltpu.roll(line, BINS + 1, 1, stride=1, stride_axis=0)
        taps[pl.ds(q * BINS, BINS), :] = turned.T[:BINS, :BINS].astype(jnp.bfloat16)
    diagonal = lax.broadcasted_iota(jnp.int32, (BINS, BINS), 0) == lax.broadcasted_iota(jnp.int32, (BINS, BINS), 1)
    sinking = jnp.sum(jnp.where(diagonal, jnp.broadcast_to(settle[...], (BINS, BINS)), 0.0), axis=1, keepdims=True)
    sinking = jnp.broadcast_to(sinking, (BINS, WIDTH))

    def fill(table, group, owner, row, weight, count):
        def one(r, _):
            number = jnp.int32(0)
            masses, total = [], jnp.float32(0.0)
            for k in range(ENTRIES):
                o = owner[k, r]
                mine = (o >= 5 * group) & (o < 5 * group + 5) & (k < count[0, r])
                w = jnp.where(mine, weight[k, r], jnp.float32(0.0))
                i = jnp.where(mine, (o - 5 * group) * ROWS + row[k, r], jnp.int32(2 * ROWS))
                number = number + jnp.where(mine, jnp.int32(1), jnp.int32(0))
                masses.append((w, mine))
                total = total + w
                index_s[table, r * ENTRIES + k] = i
            for k in range(ENTRIES):
                w, mine = masses[k]
                if table < 2:
                    w = jnp.where((number == 1) & mine, jnp.float32(1.0), w)
                mix_s[table, r * ENTRIES + k] = w
            return 0
        lax.fori_loop(0, ROWS, one, 0)

    def fill_scale(r, _):
        for side in (0, 1):
            group = 2 * side
            number, total = jnp.int32(0), jnp.float32(0.0)
            for k in range(ENTRIES):
                o = owner_s[k, r]
                mine = (o >= 5 * group) & (o < 5 * group + 5) & (k < count_s[0, r])
                number = number + jnp.where(mine, jnp.int32(1), jnp.int32(0))
                total = total + jnp.where(mine, weight_s[k, r], jnp.float32(0.0))
            scale_s[side, r] = jnp.where(number == 1, total, jnp.float32(1.0))
        return 0

    for fetch in fetches[:5]:
        fetch.wait()
    fill(2, 1, owner_s, row_s, weight_s, count_s)
    lax.fori_loop(0, ROWS, fill_scale, 0)

    def read_near(side, there):
        for copy in dep_arrivals(side, there):
            copy.wait_recv()
        moves = [
            pltpu.make_async_copy(near_int.at[side], near_int_s.at[side], own_int.at[side, 0]),
            pltpu.make_async_copy(near_weight.at[side], near_weight_s.at[side], own_int.at[side, 1]),
            pltpu.make_async_copy(near_count.at[side], near_count_s.at[side], own_int.at[side, 2]),
        ]
        for move in moves:
            move.start()
        for move in moves:
            move.wait()
        fill(side, 2 - 2 * side, near_int_s.at[side, 0], near_int_s.at[side, 1], near_weight_s.at[side],
             near_count_s.at[side])

    for side in (0, 1):
        with_neighbour(side, read_near)

    for fetch in fetches[7:]:
        fetch.wait()

    def grow(r, _):
        cells = conc_v[r]
        product = jnp.dot(taps[...], cells, preferred_element_type=jnp.float32)
        total = -sinking * cells.astype(jnp.float32)
        for q in range(4):
            total = total + rates[q, pl.ds(r, 1), :] * product[q * BINS:(q + 1) * BINS]
        base[r] = total
        return 0

    def grow_some(c):
        lax.fori_loop(c * (ROWS // CHUNKS), (c + 1) * (ROWS // CHUNKS), grow, 0, unroll=2)

    def mixed(c, table, r):
        total = jnp.zeros((GROUP, LANES), jnp.float32)
        for k in range(ENTRIES):
            place = index_s[table, r * ENTRIES + k]
            total = total + mix_s[table, r * ENTRIES + k] * held[c][place].astype(jnp.float32)
        return total

    def part_send_copy(c, side, there):
        return remote(
            sent[c].at[side], got[c].at[1 - side], part_send.at[c, side], part_recv.at[c, 1 - side], lat=there
        )

    def part_arrival(c, side, there):
        return remote(
            sent[c].at[side], got[c].at[side], part_send.at[c, side], part_recv.at[c, side], lat=there
        )

    def partials(c):
        def action(side, there):
            def one(r, _):
                sent[c][side, r] = mixed(c, side, r).astype(jnp.bfloat16)
                return 0
            lax.fori_loop(0, ROWS, one, 0, unroll=2)
            part_send_copy(c, side, there).start()
        for side in (0, 1):
            with_neighbour(side, action)

    def remap(c):
        g, h = c // HALVES, c % HALVES
        for side in (0, 1):
            with_neighbour(side, lambda side, there: part_arrival(c, side, there).wait_recv())

        def one(r, _):
            total = mixed(c, 2, r)
            for side in (0, 1):
                total = total + scale_s[side, r] * got[c][side, r].astype(jnp.float32)
            remapped[g][r, :, pl.ds(h * LANES, LANES)] = total.astype(jnp.bfloat16)
            return 0

        lax.fori_loop(0, ROWS, one, 0, unroll=2)

    def strip_sends(g):
        return [
            remote(remapped[g].at[:, :, pl.ds(0, STRIP)], strips[g].at[1],
                   strip_send.at[g, 0], strip_recv.at[g, 1], lon=west),
            remote(remapped[g].at[:, :, pl.ds(WIDTH - STRIP, STRIP)], strips[g].at[0],
                   strip_send.at[g, 1], strip_recv.at[g, 0], lon=east),
        ]

    def strip_arrivals(g):
        return [
            remote(remapped[g].at[:, :, pl.ds(0, STRIP)], strips[g].at[side],
                   strip_send.at[g, side], strip_recv.at[g, side], lon=west)
            for side in (0, 1)
        ]

    span = WIDTH + 2 * STRIP

    def shifted(g, r):
        line = jnp.concatenate([strips[g][0, r], remapped[g][r], strips[g][1, r]], axis=1).astype(jnp.float32)
        step = offset_s[r]
        line = pltpu.roll(line, jnp.where(step < 0, step + span, step), 1)
        beside = pltpu.roll(line, 1, 1) + pltpu.roll(line, span - 1, 1)
        return line[:, STRIP:STRIP + WIDTH], beside[:, STRIP:STRIP + WIDTH]

    def edge_copy(g, side, there):
        return remote(
            ends[g].at[side], edges[g].at[1 - side], edge_send.at[g, side], edge_recv.at[g, 1 - side], lat=there
        )

    def edge_arrival(g, side, there):
        return remote(
            ends[g].at[side], edges[g].at[side], edge_send.at[g, side], edge_recv.at[g, side], lat=there
        )

    def outer_rows(g):
        for copy in strip_arrivals(g):
            copy.wait_recv()

        def action(side, there):
            center, _ = shifted(g, 0 if side == 0 else ROWS - 1)
            ends[g][side] = center.astype(jnp.bfloat16)
            edge_copy(g, side, there).start()

        for side in (0, 1):
            with_neighbour(side, action)

        def one(r, _):
            centers[g][r + 1], besides[g][r] = shifted(g, r)
            return 0

        lax.fori_loop(0, ROWS, one, 0, unroll=4)

    def finish(g):
        for side in (0, 1):
            with_neighbour(side, lambda side, there: edge_arrival(g, side, there).wait_recv())
        centers[g][0] = edges[g][0].astype(jnp.float32)
        centers[g][ROWS + 1] = edges[g][1].astype(jnp.float32)
        bins = pl.ds(g * GROUP, GROUP)

        def one(r, _):
            center = centers[g][r + 1]
            around = (centers[g][r] + centers[g][r + 2]) + besides[g][r]
            base[r, bins, :] = base[r, bins, :] + center + kappa[pl.ds(r, 1), :] * (around - 4.0 * center)
            return 0

        lax.fori_loop(0, ROWS, one, 0, unroll=4)

    for c in range(CHUNKS):
        for which in (0, 1):
            raw_arrival(c, which).wait_recv()
        forward(c).start()
        if c + AHEAD < CHUNKS:
            for copy in raw_sends(c + AHEAD):
                copy.start()
        own_copy(c).wait()
        for which in (2, 3):
            raw_arrival(c, which).wait_recv()
        partials(c)
        grow_some(c)
        if c >= 1:
            remap(c - 1)
            if (c - 1) % HALVES == HALVES - 1:
                for copy in strip_sends((c - 1) // HALVES):
                    copy.start()
        if c % HALVES == 0 and c // HALVES >= 2:
            outer_rows(c // HALVES - 2)
        if c % HALVES == 0 and c // HALVES >= 3:
            finish(c // HALVES - 3)
    if GROUPS >= 3:
        finish(GROUPS - 3)
    outer_rows(GROUPS - 2)
    remap(CHUNKS - 1)
    for copy in strip_sends(GROUPS - 1):
        copy.start()
    finish(GROUPS - 2)
    outer_rows(GROUPS - 1)
    finish(GROUPS - 1)

    for c in range(CHUNKS):
        for copy in raw_sends(c):
            copy.wait_send()
        forward(c).wait_send()
        for side in (0, 1):
            with_neighbour(side, lambda side, there: part_send_copy(c, side, there).wait_send())
    for g in range(GROUPS):
        for copy in strip_sends(g):
            copy.wait_send()
        for side in (0, 1):
            with_neighbour(side, lambda side, there: edge_copy(g, side, there).wait_send())

    def dep_sent(side, there):
        for copy in dep_sends(side, there):
            copy.wait_send()

    for side in (0, 1):
        with_neighbour(side, dep_sent)


def solution(mesh):
    n_lat, n_lon = mesh.shape["lat"], mesh.shape["lon"]

    def body(conc, dep_owner, dep_row, dep_weight, dep_count, zonal_offset, agg_rates, toeplitz, settle, kappa):
        owner, row, weight = dep_owner[0].T, dep_row[0].T, dep_weight[0].T
        hbm = pl.BlockSpec(memory_space=pltpu.HBM)
        bf16, f32, i32 = jnp.bfloat16, jnp.float32, jnp.int32
        dma = pltpu.SemaphoreType.DMA
        return pl.pallas_call(
            functools.partial(kernel, n_lat, n_lon),
            out_shape=jax.ShapeDtypeStruct((ROWS, BINS, WIDTH), f32),
            in_specs=[hbm] * 10,
            out_specs=pl.BlockSpec(memory_space=pltpu.VMEM),
            scratch_shapes=[
                pltpu.SMEM((ENTRIES, ROWS), i32),
                pltpu.SMEM((ENTRIES, ROWS), i32),
                pltpu.SMEM((ENTRIES, ROWS), f32),
                pltpu.SMEM((1, ROWS), i32),
                pltpu.SMEM((ROWS,), i32),
                pltpu.VMEM((4, ROWS, WIDTH), f32),
                pltpu.VMEM((4, 2 * BINS - 1), bf16),
                pltpu.VMEM((1, BINS), f32),
                pltpu.VMEM((ROWS, WIDTH), f32),
                pltpu.VMEM((ROWS, BINS, WIDTH), bf16),
                pltpu.VMEM((4 * BINS, BINS), bf16),
                pltpu.VMEM((4, 2 * BINS), f32),
                pltpu.VMEM((2, 2, ENTRIES, ROWS), i32),
                pltpu.VMEM((2, ENTRIES, ROWS), f32),
                pltpu.VMEM((2, 1, ROWS), i32),
                dma((10,)),
                dma((2, 3)),
                pltpu.SMEM((2, 2, ENTRIES, ROWS), i32),
                pltpu.SMEM((2, ENTRIES, ROWS), f32),
                pltpu.SMEM((2, 1, ROWS), i32),
                pltpu.SMEM((3, ROWS * ENTRIES), i32),
                pltpu.SMEM((3, ROWS * ENTRIES), f32),
                pltpu.SMEM((2, ROWS), f32),
            ]
            + [pltpu.VMEM((5 * ROWS, GROUP, LANES), bf16) for _ in range(CHUNKS)]
            + [pltpu.VMEM((2, ROWS, GROUP, LANES), bf16) for _ in range(2 * CHUNKS)]
            + [pltpu.VMEM((ROWS, GROUP, WIDTH), bf16) for _ in range(GROUPS)]
            + [pltpu.VMEM((2, ROWS, GROUP, STRIP), bf16) for _ in range(GROUPS)]
            + [pltpu.VMEM((2, GROUP, WIDTH), bf16) for _ in range(2 * GROUPS)]
            + [pltpu.VMEM((ROWS + 2, GROUP, WIDTH), f32) for _ in range(GROUPS)]
            + [pltpu.VMEM((ROWS, GROUP, WIDTH), f32) for _ in range(GROUPS)]
            + [
                dma((2, 4)), dma((2, 4)),
                dma((CHUNKS, 4)), dma((CHUNKS, 4)),
                dma((CHUNKS, 2)), dma((CHUNKS, 2)),
                dma((GROUPS, 2)), dma((GROUPS, 2)),
                dma((GROUPS, 2)), dma((GROUPS, 2)),
                dma((CHUNKS,)),
            ],
            compiler_params=pltpu.CompilerParams(
                collective_id=0, has_side_effects=True, vmem_limit_bytes=40 << 20
            ),
            name="remap_step",
        )(
            *[
                pltpu.with_memory_space_constraint(operand, pltpu.HBM)
                for operand in (
                    conc, owner, row, weight, dep_count, zonal_offset, agg_rates, toeplitz,
                    settle.reshape(1, BINS), kappa,
                )
            ]
        )

    return jax.shard_map(
        body,
        mesh=mesh,
        in_specs=(
            P("lat", None, "lon"),
            P("lon", "lat", None),
            P("lon", "lat", None),
            P("lon", "lat", None),
            P("lon", "lat"),
            P("lat"),
            P(None, "lat", "lon"),
            P(),
            P(),
            P("lat", "lon"),
        ),
        out_specs=P("lat", None, "lon"),
        check_vma=False,
    )
```

```python
import functools

import jax
import jax.numpy as jnp
from jax import lax
from jax.experimental import pallas as pl
from jax.experimental.pallas import tpu as pltpu
from jax.sharding import PartitionSpec as P

MESH = pl.DeviceIdType.MESH
ROWS = 32
BINS = 64
WIDTH = 256
ENTRIES = 4
GROUP = 16
GROUPS = BINS // GROUP
HALVES = 2
LANES = WIDTH // HALVES
CHUNKS = GROUPS * HALVES
BLOCK = 8
LAG = 2
TILE = 128


def kernel(
    n_lat, n_lon,
    conc, owner_h, row_h, weight_h, count_h, offset_h, rates_h, toeplitz_h, settle_h, kappa_h,
    base,
    owner_v, row_v, weight_v, count_v, offset_v, rates, toeplitz, settle, kappa,
    conc_v, taps, toep_v, stencil, places_v, mixes_v, near_places, near_mixes, places, mixes,
    fetch_sem, table_sem,
    *rest,
):
    held = rest[0:CHUNKS]
    sent = rest[CHUNKS:2 * CHUNKS]
    got = rest[2 * CHUNKS:3 * CHUNKS]
    rest = rest[3 * CHUNKS:]
    remapped, packs, halos, edges, moved = (rest[i * GROUPS:(i + 1) * GROUPS] for i in range(5))
    (dep_send, dep_recv, raw_send, raw_recv, part_send, part_recv,
     halo_send, halo_recv, edge_send, edge_recv, local_sem) = rest[5 * GROUPS:]

    lat = lax.axis_index("lat")
    lon = lax.axis_index("lon")
    core = lax.rem(lon, 2)
    chip = lon - core

    def at_lon(value):
        return lax.rem(value + 2 * n_lon, n_lon)

    sibling = chip + 1 - core
    after = at_lon(chip + 2)
    before = at_lon(chip - 1)
    beside_lon = (at_lon(lon - 1), at_lon(lon + 1))

    fetches = [
        pltpu.make_async_copy(src, dst, fetch_sem.at[i])
        for i, (src, dst) in enumerate([
            (owner_h, owner_v), (row_h, row_v), (weight_h, weight_v), (count_h, count_v), (offset_h, offset_v),
            (toeplitz_h, toeplitz), (settle_h, settle), (rates_h, rates), (kappa_h, kappa), (conc, conc_v),
        ])
    ]
    for fetch in fetches:
        fetch.start()

    def with_neighbour(side, action):
        inside = lat > 0 if side == 0 else lat < n_lat - 1
        pl.when(inside)(functools.partial(action, side, lat - 1 if side == 0 else lat + 1))

    barrier = pltpu.get_barrier_semaphore()
    for step in (-2, -1, 1, 2):
        pl.semaphore_signal(barrier, inc=1, device_id={"lon": at_lon(lon + step)}, device_id_type=MESH)

    def greet(side, there):
        pl.semaphore_signal(barrier, inc=1, device_id={"lat": there}, device_id_type=MESH)
        for across in beside_lon:
            pl.semaphore_signal(barrier, inc=1, device_id={"lat": there, "lon": across}, device_id_type=MESH)

    for side in (0, 1):
        with_neighbour(side, greet)

    for fetch in fetches[:5]:
        fetch.wait()
    owner, weight = owner_v[...], weight_v[...]
    live = lax.broadcasted_iota(jnp.int32, (ENTRIES, ROWS), 0) < count_v[...]
    places_v[...] = jnp.zeros_like(places_v)
    mixes_v[...] = jnp.zeros_like(mixes_v)
    for group, table in ((0, 0), (2, 1), (1, 2)):
        mine = live & (owner >= 5 * group) & (owner < 5 * group + 5)
        mass = jnp.where(mine, weight, 0.0)
        places_v[table, pl.ds(0, ENTRIES), :] = jnp.where(mine, (owner - 5 * group) * ROWS + row_v[...], 2 * ROWS)
        places_v[table, pl.ds(ENTRIES, 1), :] = offset_v[...]
        if group != 1:
            single = jnp.sum(mine.astype(jnp.int32), axis=0, keepdims=True) == 1
            mixes_v[2, pl.ds(ENTRIES + table, 1), :] = jnp.where(single, jnp.sum(mass, axis=0, keepdims=True), 1.0)
            mass = jnp.where(mine & single, 1.0, mass)
        mixes_v[table, pl.ds(0, ENTRIES), :] = mass
    own_tables = [
        pltpu.make_async_copy(places_v.at[2], places.at[2], table_sem.at[2, 0]),
        pltpu.make_async_copy(mixes_v.at[2], mixes.at[2], table_sem.at[2, 1]),
    ]
    for move in own_tables:
        move.start()

    def remote(src, dst, send, recv, **where):
        return pltpu.make_async_remote_copy(
            src_ref=src, dst_ref=dst, send_sem=send, recv_sem=recv, device_id=where, device_id_type=MESH
        )

    def window(c):
        g, h = c // HALVES, c % HALVES
        return conc.at[:, pl.ds(g * GROUP, GROUP), pl.ds(h * LANES, LANES)]

    def slot(c, number):
        return held[c].at[pl.ds(number * ROWS, ROWS)]

    def raw_sends(c):
        return [
            remote(window(c), slot(c, core), raw_send.at[c, 0], raw_recv.at[c, core], lon=after),
            remote(window(c), slot(c, core + 3), raw_send.at[c, 1], raw_recv.at[c, core], lon=before),
            remote(window(c), slot(c, 1 + 2 * core), raw_send.at[c, 2], raw_recv.at[c, 2], lon=sibling),
        ]

    far = 3 * core

    def raw_arrival(c, which):
        number = (far, far + 1, 3 - 2 * core, 4 - 4 * core)[which]
        return remote(window(c), slot(c, number), raw_send.at[c, 3], raw_recv.at[c, which], lon=sibling)

    def forward(c):
        return remote(
            slot(c, 1 + 2 * core), slot(c, 4 * core), raw_send.at[c, 3], raw_recv.at[c, 3], lon=sibling
        )

    def own_copy(c):
        return pltpu.make_async_copy(window(c), slot(c, 2), local_sem.at[c])

    def dep_copies(side, into, there):
        return [
            remote(places_v.at[side], near_places.at[into], dep_send.at[side, 0], dep_recv.at[into, 0], lat=there),
            remote(mixes_v.at[side], near_mixes.at[into], dep_send.at[side, 1], dep_recv.at[into, 1], lat=there),
        ]

    def dep_start(side, there):
        for copy in dep_copies(side, 1 - side, there):
            copy.start()

    pl.semaphore_wait(barrier, 4 + 3 * (jnp.where(lat > 0, 1, 0) + jnp.where(lat < n_lat - 1, 1, 0)))
    for side in (0, 1):
        with_neighbour(side, dep_start)
    for c in range(CHUNKS):
        for copy in raw_sends(c):
            copy.start()
    for c in range(CHUNKS):
        own_copy(c).start()

    for fetch in fetches[5:]:
        fetch.wait()
    toep_v[...] = jnp.zeros_like(toep_v)
    toep_v[:, pl.ds(0, 2 * BINS - 1)] = toeplitz[...].astype(jnp.float32)
    for q in range(4):
        line = jnp.broadcast_to(toep_v[pl.ds(q, 1), :], (2 * BINS, 2 * BINS))
        turned = pltpu.roll(line, BINS + 1, 1, stride=1, stride_axis=0)
        taps[pl.ds(q * BINS, BINS), :] = turned.T[:BINS, :BINS].astype(jnp.bfloat16)
    diagonal = lax.broadcasted_iota(jnp.int32, (BINS, BINS), 0) == lax.broadcasted_iota(jnp.int32, (BINS, BINS), 1)
    sinking = jnp.sum(jnp.where(diagonal, jnp.broadcast_to(settle[...], (BINS, BINS)), 0.0), axis=1, keepdims=True)
    sinking = jnp.broadcast_to(sinking, (BINS, WIDTH))

    apart = lax.broadcasted_iota(jnp.int32, (3 * TILE, WIDTH), 0) - lax.broadcasted_iota(
        jnp.int32, (3 * TILE, WIDTH), 1
    )
    near = (apart == 1) | (apart == -1) | (apart == 3 * TILE - 1)
    stencil[...] = jnp.where(near, 1.0, jnp.where(apart == 0, -4.0, 0.0)).astype(jnp.bfloat16)

    for move in own_tables:
        move.wait()

    def read_near(side, there):
        for copy in dep_copies(side, side, there):
            copy.wait_recv()
        moves = [
            pltpu.make_async_copy(near_places.at[side], places.at[side], table_sem.at[side, 0]),
            pltpu.make_async_copy(near_mixes.at[side], mixes.at[side], table_sem.at[side, 1]),
        ]
        for move in moves:
            move.start()
        for move in moves:
            move.wait()

    for side in (0, 1):
        with_neighbour(side, read_near)

    def clear(side):
        def action():
            for c in range(CHUNKS):
                got[c][side] = jnp.zeros((ROWS, GROUP, LANES), jnp.bfloat16)
            for g in range(GROUPS):
                edges[g][side] = jnp.zeros((GROUP, WIDTH), jnp.bfloat16)
                for across in (0, 1):
                    halos[g][across, 2 * side] = jnp.zeros((GROUP, TILE), jnp.bfloat16)
            places[side, ENTRIES, ROWS - 1 if side == 0 else 0] = jnp.int32(0)
        pl.when(lat == (0 if side == 0 else n_lat - 1))(action)

    for side in (0, 1):
        clear(side)

    def grow(r, _):
        cells = conc_v[r]
        product = jnp.dot(taps[...], cells, preferred_element_type=jnp.float32)
        total = -sinking * cells.astype(jnp.float32)
        for q in range(4):
            total = total + rates[q, pl.ds(r, 1), :] * product[q * BINS:(q + 1) * BINS]
        base[r] = total
        return 0

    def grow_some(c):
        share = 2 * ROWS // CHUNKS
        if c < CHUNKS // 2:
            lax.fori_loop(c * share, (c + 1) * share, grow, 0, unroll=2)

    def mixed(c, table, r):
        total = None
        for k in range(ENTRIES):
            term = mixes[table, k, r] * held[c][places[table, k, r]].astype(jnp.float32)
            total = term if total is None else total + term
        return total

    def part_copy(c, side, into, there):
        return remote(
            sent[c].at[side], got[c].at[into], part_send.at[c, side], part_recv.at[c, into], lat=there
        )

    def partials(c):
        def action(side, there):
            def one(r, _):
                sent[c][side, r] = mixed(c, side, r).astype(jnp.bfloat16)
                return 0
            lax.fori_loop(0, ROWS, one, 0, unroll=4)
            part_copy(c, side, 1 - side, there).start()
        for side in (0, 1):
            with_neighbour(side, action)

    lane = lax.broadcasted_iota(jnp.int32, (GROUP, TILE), 1)

    def wanted(step):
        return jnp.where(step > -1, step + 1, 0), jnp.where(step < 1, 1 - step, 0)

    def remap(c):
        g, h = c // HALVES, c % HALVES
        for side in (0, 1):
            with_neighbour(side, lambda side, there: part_copy(c, side, side, there).wait_recv())
        sides = {0: [0], 1: [1]}[h] if HALVES == 2 else [0, 1]

        def one(r, packed):
            total = mixed(c, 2, r)
            for side in (0, 1):
                total = total + mixes[2, ENTRIES + side, r] * got[c][side, r].astype(jnp.float32)
            rounded = total.astype(jnp.bfloat16)
            remapped[g][r, :, pl.ds(h * LANES, LANES)] = rounded
            rounded = rounded.astype(jnp.float32)
            before_row, after_row = wanted(places[2, ENTRIES, r])
            start = 4 * r + before_row
            found = []
            for side, kept in zip(sides, packed):
                tile = rounded[:, :TILE] if side == 0 else rounded[:, LANES - TILE:]
                if side == 0:
                    here = (lane >= start) & (lane < start + after_row)
                else:
                    here = (lane >= 4 * r) & (lane < start)
                found.append(jnp.where(here, pltpu.roll(tile, lax.rem(start, TILE), 1), kept))
            return tuple(found)

        empty = jnp.zeros((GROUP, TILE), jnp.float32)
        packed = lax.fori_loop(0, ROWS, one, (empty,) * len(sides), unroll=4)
        for side, tile in zip(sides, packed):
            packs[g][side] = tile.astype(jnp.bfloat16)

    def halo_copy(g, across, up, into_across, into_up, where):
        return remote(
            packs[g].at[across], halos[g].at[into_across, into_up],
            halo_send.at[g, across, up], halo_recv.at[g, into_across, into_up], **where
        )

    def edge_copy(g, side, into, there):
        row = 0 if side == 0 else ROWS - 1
        return remote(
            remapped[g].at[row], edges[g].at[into], edge_send.at[g, side], edge_recv.at[g, into], lat=there
        )

    def outgoing(g, act):
        for across in (0, 1):
            act(halo_copy(g, across, 1, 1 - across, 1, {"lon": beside_lon[across]}))

        def action(side, there):
            act(edge_copy(g, side, 1 - side, there))
            for across in (0, 1):
                act(halo_copy(
                    g, across, 2 * side, 1 - across, 2 - 2 * side, {"lat": there, "lon": beside_lon[across]}
                ))

        for side in (0, 1):
            with_neighbour(side, action)

    def incoming(g):
        for across in (0, 1):
            halo_copy(g, across, 1, across, 1, {"lon": beside_lon[across]}).wait_recv()

        def action(side, there):
            edge_copy(g, side, side, there).wait_recv()
            for across in (0, 1):
                halo_copy(
                    g, across, 2 * side, across, 2 * side, {"lat": there, "lon": beside_lon[across]}
                ).wait_recv()

        for side in (0, 1):
            with_neighbour(side, action)

    def shifted(line, packed, r, step):
        left, right = line[:, :TILE], line[:, TILE:]
        turn = jnp.where(step < 0, step + TILE, step)
        low, high = lane < step, lane >= TILE + step
        halo = pltpu.roll(packed, lax.rem(turn + 2 * TILE - 4 * r - wanted(step)[0], TILE), 1)
        left, right = pltpu.roll(left, turn, 1), pltpu.roll(right, turn, 1)

        def pick(prior, tile, later):
            return jnp.where(low, prior, jnp.where(high, later, tile))

        tiles = pick(halo, left, right), pick(left, right, halo), pick(right, halo, left)
        return jnp.concatenate(tiles, axis=1).astype(jnp.bfloat16)

    def finish(g):
        incoming(g)

        def packed(up):
            return halos[g][0, up].astype(jnp.float32) + halos[g][1, up].astype(jnp.float32)

        middle = packed(1)

        def shift(r, _):
            moved[g][r + 1] = shifted(remapped[g][r].astype(jnp.float32), middle, r, places[2, ENTRIES, r])
            return 0

        lax.fori_loop(0, ROWS, shift, 0, unroll=4)
        for side in (0, 1):
            r = ROWS - 1 if side == 0 else 0
            moved[g][(ROWS + 1) * side] = shifted(
                edges[g][side].astype(jnp.float32), packed(2 * side), jnp.int32(r), places[side, ENTRIES, r]
            )
        bins = pl.ds(g * GROUP, GROUP)

        def block(n, _):
            first = n * BLOCK
            lines = moved[g][pl.ds(first + 1, BLOCK)].reshape(BLOCK * GROUP, 3 * TILE)
            along = jnp.dot(lines, stencil[...], preferred_element_type=jnp.float32)
            for i in range(BLOCK):
                r = first + i
                center, above, below = (
                    moved[g][r + d, :, pl.ds(0, WIDTH)].astype(jnp.float32) for d in (1, 0, 2)
                )
                total = base[r, bins, :] + center
                base[r, bins, :] = total + kappa[pl.ds(r, 1), :] * (
                    (above + below) + along[i * GROUP:(i + 1) * GROUP]
                )
            return 0

        lax.fori_loop(0, ROWS // BLOCK, block, 0)

    def settle_chunk(c):
        remap(c)
        if c % HALVES == HALVES - 1:
            outgoing(c // HALVES, lambda copy: copy.start())

    for c in range(CHUNKS):
        for which in (0, 1):
            raw_arrival(c, which).wait_recv()
        forward(c).start()
        grow_some(c)
        own_copy(c).wait()
        for which in (2, 3):
            raw_arrival(c, which).wait_recv()
        partials(c)
        if c >= LAG:
            settle_chunk(c - LAG)
    finished = 0
    for c in range(CHUNKS - LAG, CHUNKS):
        settle_chunk(c)
        if finished < (c - 1) // HALVES:
            finish(finished)
            finished += 1
    for g in range(finished, GROUPS):
        finish(g)

    for c in range(CHUNKS):
        for copy in raw_sends(c):
            copy.wait_send()
        forward(c).wait_send()
        for side in (0, 1):
            with_neighbour(side, lambda side, there: part_copy(c, side, 1 - side, there).wait_send())
    for g in range(GROUPS):
        outgoing(g, lambda copy: copy.wait_send())

    def dep_sent(side, there):
        for copy in dep_copies(side, 1 - side, there):
            copy.wait_send()

    for side in (0, 1):
        with_neighbour(side, dep_sent)


def solution(mesh):
    n_lat, n_lon = mesh.shape["lat"], mesh.shape["lon"]

    def body(conc, dep_owner, dep_row, dep_weight, dep_count, zonal_offset, agg_rates, toeplitz, settle, kappa):
        owner, row, weight = dep_owner[0].T, dep_row[0].T, dep_weight[0].T
        hbm = pl.BlockSpec(memory_space=pltpu.HBM)
        bf16, f32, i32 = jnp.bfloat16, jnp.float32, jnp.int32
        dma = pltpu.SemaphoreType.DMA
        return pl.pallas_call(
            functools.partial(kernel, n_lat, n_lon),
            out_shape=jax.ShapeDtypeStruct((ROWS, BINS, WIDTH), f32),
            in_specs=[hbm] * 10,
            out_specs=pl.BlockSpec(memory_space=pltpu.VMEM),
            scratch_shapes=[
                pltpu.VMEM((ENTRIES, ROWS), i32),
                pltpu.VMEM((ENTRIES, ROWS), i32),
                pltpu.VMEM((ENTRIES, ROWS), f32),
                pltpu.VMEM((1, ROWS), i32),
                pltpu.VMEM((1, ROWS), i32),
                pltpu.VMEM((4, ROWS, WIDTH), f32),
                pltpu.VMEM((4, 2 * BINS - 1), bf16),
                pltpu.VMEM((1, BINS), f32),
                pltpu.VMEM((ROWS, WIDTH), f32),
                pltpu.VMEM((ROWS, BINS, WIDTH), bf16),
                pltpu.VMEM((4 * BINS, BINS), bf16),
                pltpu.VMEM((4, 2 * BINS), f32),
                pltpu.VMEM((3 * TILE, WIDTH), bf16),
                pltpu.VMEM((3, 8, ROWS), i32),
                pltpu.VMEM((3, 8, ROWS), f32),
                pltpu.VMEM((2, 8, ROWS), i32),
                pltpu.VMEM((2, 8, ROWS), f32),
                pltpu.SMEM((3, 8, ROWS), i32),
                pltpu.SMEM((3, 8, ROWS), f32),
                dma((10,)),
                dma((3, 2)),
            ]
            + [pltpu.VMEM((5 * ROWS, GROUP, LANES), bf16) for _ in range(CHUNKS)]
            + [pltpu.VMEM((2, ROWS, GROUP, LANES), bf16) for _ in range(2 * CHUNKS)]
            + [pltpu.VMEM((ROWS, GROUP, WIDTH), bf16) for _ in range(GROUPS)]
            + [pltpu.VMEM((2, GROUP, TILE), bf16) for _ in range(GROUPS)]
            + [pltpu.VMEM((2, 3, GROUP, TILE), bf16) for _ in range(GROUPS)]
            + [pltpu.VMEM((2, GROUP, WIDTH), bf16) for _ in range(GROUPS)]
            + [pltpu.VMEM((ROWS + 2, GROUP, 3 * TILE), bf16) for _ in range(GROUPS)]
            + [
                dma((2, 2)), dma((2, 2)),
                dma((CHUNKS, 4)), dma((CHUNKS, 4)),
                dma((CHUNKS, 2)), dma((CHUNKS, 2)),
                dma((GROUPS, 2, 3)), dma((GROUPS, 2, 3)),
                dma((GROUPS, 2)), dma((GROUPS, 2)),
                dma((CHUNKS,)),
            ],
            compiler_params=pltpu.CompilerParams(
                collective_id=0, has_side_effects=True, vmem_limit_bytes=40 << 20
            ),
            name="remap_step",
        )(
            *[
                pltpu.with_memory_space_constraint(operand, pltpu.HBM)
                for operand in (
                    conc, owner, row, weight, dep_count, zonal_offset.reshape(1, ROWS), agg_rates, toeplitz,
                    settle.reshape(1, BINS), kappa,
                )
            ]
        )

    return jax.shard_map(
        body,
        mesh=mesh,
        in_specs=(
            P("lat", None, "lon"),
            P("lon", "lat", None),
            P("lon", "lat", None),
            P("lon", "lat", None),
            P("lon", "lat"),
            P("lat"),
            P(None, "lat", "lon"),
            P(),
            P(),
            P("lat", "lon"),
        ),
        out_specs=P("lat", None, "lon"),
        check_vma=False,
    )
```

```python
import functools

import jax
import jax.numpy as jnp
from jax import lax
from jax.experimental import pallas as pl
from jax.experimental.pallas import tpu as pltpu
from jax.sharding import PartitionSpec as P

MESH = pl.DeviceIdType.MESH
ROWS = 32
BINS = 64
WIDTH = 256
ENTRIES = 4
GROUP = 16
GROUPS = BINS // GROUP
HALVES = 2
LANES = WIDTH // HALVES
CHUNKS = GROUPS * HALVES
BLOCK = 16
LAG = 3
TILE = 128


def kernel(
    n_lat, n_lon,
    conc, owner_h, row_h, weight_h, count_h, offset_h, rates_h, toeplitz_h, settle_h, kappa_h,
    base,
    owner_v, row_v, weight_v, count_v, offset_v, rates, toeplitz, settle, kappa,
    conc_v, taps, toep_v, stencil, places_v, mixes_v, near_places, near_mixes, places, mixes,
    fetch_sem, table_sem,
    *rest,
):
    held = rest[0:CHUNKS]
    sent = rest[CHUNKS:2 * CHUNKS]
    got = rest[2 * CHUNKS:3 * CHUNKS]
    rest = rest[3 * CHUNKS:]
    remapped, packs, halos, corners, edges, moved = (
        rest[i * GROUPS:(i + 1) * GROUPS] for i in range(6)
    )
    (dep_send, dep_recv, raw_send, raw_recv, part_send, part_recv,
     halo_send, halo_recv, corner_send, corner_recv, edge_send, edge_recv, local_sem) = rest[6 * GROUPS:]

    lat = lax.axis_index("lat")
    lon = lax.axis_index("lon")
    core = lax.rem(lon, 2)
    chip = lon - core

    def at_lon(value):
        return lax.rem(value + 2 * n_lon, n_lon)

    sibling = chip + 1 - core
    after = at_lon(chip + 2)
    before = at_lon(chip - 1)
    beside_lon = (at_lon(lon - 1), at_lon(lon + 1))

    def with_neighbour(side, action):
        inside = lat > 0 if side == 0 else lat < n_lat - 1
        pl.when(inside)(functools.partial(action, side, lat - 1 if side == 0 else lat + 1))

    barrier = pltpu.get_barrier_semaphore()
    for step in (-2, -1, 1, 2):
        pl.semaphore_signal(barrier, inc=1, device_id={"lon": at_lon(lon + step)}, device_id_type=MESH)

    def greet(side, there):
        pl.semaphore_signal(barrier, inc=1, device_id={"lat": there}, device_id_type=MESH)
        for across in beside_lon:
            pl.semaphore_signal(barrier, inc=1, device_id={"lat": there, "lon": across}, device_id_type=MESH)

    for side in (0, 1):
        with_neighbour(side, greet)

    fetches = [
        pltpu.make_async_copy(src, dst, fetch_sem.at[i])
        for i, (src, dst) in enumerate([
            (owner_h, owner_v), (row_h, row_v), (weight_h, weight_v), (count_h, count_v), (offset_h, offset_v),
            (toeplitz_h, toeplitz), (settle_h, settle), (rates_h, rates), (kappa_h, kappa), (conc, conc_v),
        ])
    ]
    for fetch in fetches:
        fetch.start()

    def remote(src, dst, send, recv, **where):
        return pltpu.make_async_remote_copy(
            src_ref=src, dst_ref=dst, send_sem=send, recv_sem=recv, device_id=where, device_id_type=MESH
        )

    def window(c):
        g, h = c // HALVES, c % HALVES
        return conc.at[:, pl.ds(g * GROUP, GROUP), pl.ds(h * LANES, LANES)]

    def slot(c, number):
        return held[c].at[pl.ds(number * ROWS, ROWS)]

    def raw_sends(c):
        return [
            remote(window(c), slot(c, core), raw_send.at[c, 0], raw_recv.at[c, core], lon=after),
            remote(window(c), slot(c, core + 3), raw_send.at[c, 1], raw_recv.at[c, core], lon=before),
            remote(window(c), slot(c, 1 + 2 * core), raw_send.at[c, 2], raw_recv.at[c, 2], lon=sibling),
        ]

    far = 3 * core

    def raw_arrival(c, which):
        number = (far, far + 1, 3 - 2 * core, 4 - 4 * core)[which]
        return remote(window(c), slot(c, number), raw_send.at[c, 3], raw_recv.at[c, which], lon=sibling)

    def forward(c):
        return remote(
            slot(c, 1 + 2 * core), slot(c, 4 * core), raw_send.at[c, 3], raw_recv.at[c, 3], lon=sibling
        )

    def own_copy(c):
        return pltpu.make_async_copy(window(c), slot(c, 2), local_sem.at[c])

    def dep_copies(side, into, there):
        return [
            remote(places_v.at[side], near_places.at[into], dep_send.at[side, 0], dep_recv.at[into, 0], lat=there),
            remote(mixes_v.at[side], near_mixes.at[into], dep_send.at[side, 1], dep_recv.at[into, 1], lat=there),
        ]

    def dep_start(side, there):
        for copy in dep_copies(side, 1 - side, there):
            copy.start()

    pl.semaphore_wait(barrier, 4 + 3 * (jnp.where(lat > 0, 1, 0) + jnp.where(lat < n_lat - 1, 1, 0)))
    for c in range(CHUNKS):
        for copy in raw_sends(c):
            copy.start()
    for c in range(CHUNKS):
        own_copy(c).start()

    for fetch in fetches[:5]:
        fetch.wait()
    owner, weight = owner_v[...], weight_v[...]
    live = lax.broadcasted_iota(jnp.int32, (ENTRIES, ROWS), 0) < count_v[...]
    places_v[...] = jnp.zeros_like(places_v)
    mixes_v[...] = jnp.zeros_like(mixes_v)
    for group, table in ((0, 0), (2, 1), (1, 2)):
        mine = live & (owner >= 5 * group) & (owner < 5 * group + 5)
        mass = jnp.where(mine, weight, 0.0)
        places_v[table, pl.ds(0, ENTRIES), :] = jnp.where(mine, (owner - 5 * group) * ROWS + row_v[...], 2 * ROWS)
        places_v[table, pl.ds(ENTRIES, 1), :] = offset_v[...]
        if group != 1:
            single = jnp.sum(mine.astype(jnp.int32), axis=0, keepdims=True) == 1
            mixes_v[2, pl.ds(ENTRIES + table, 1), :] = jnp.where(single, jnp.sum(mass, axis=0, keepdims=True), 1.0)
            mass = jnp.where(mine & single, 1.0, mass)
        mixes_v[table, pl.ds(0, ENTRIES), :] = mass
    own_tables = [
        pltpu.make_async_copy(places_v.at[2], places.at[2], table_sem.at[2, 0]),
        pltpu.make_async_copy(mixes_v.at[2], mixes.at[2], table_sem.at[2, 1]),
    ]
    for move in own_tables:
        move.start()

    for side in (0, 1):
        with_neighbour(side, dep_start)
    for fetch in fetches[5:]:
        fetch.wait()
    toep_v[...] = jnp.zeros_like(toep_v)
    toep_v[:, pl.ds(0, 2 * BINS - 1)] = toeplitz[...].astype(jnp.float32)
    for q in range(4):
        line = jnp.broadcast_to(toep_v[pl.ds(q, 1), :], (2 * BINS, 2 * BINS))
        turned = pltpu.roll(line, BINS + 1, 1, stride=1, stride_axis=0)
        taps[pl.ds(q * BINS, BINS), :] = turned.T[:BINS, :BINS].astype(jnp.bfloat16)
    diagonal = lax.broadcasted_iota(jnp.int32, (BINS, BINS), 0) == lax.broadcasted_iota(jnp.int32, (BINS, BINS), 1)
    sinking = jnp.sum(jnp.where(diagonal, jnp.broadcast_to(settle[...], (BINS, BINS)), 0.0), axis=1, keepdims=True)
    sinking = jnp.broadcast_to(sinking, (BINS, WIDTH))

    apart = lax.broadcasted_iota(jnp.int32, (3 * TILE, WIDTH), 0) - lax.broadcasted_iota(
        jnp.int32, (3 * TILE, WIDTH), 1
    )
    near = (apart == 1) | (apart == -1) | (apart == 3 * TILE - 1)
    stencil[...] = jnp.where(near, 1.0, jnp.where(apart == 0, -4.0, 0.0)).astype(jnp.bfloat16)

    for move in own_tables:
        move.wait()

    def read_near(side, there):
        for copy in dep_copies(side, side, there):
            copy.wait_recv()
        moves = [
            pltpu.make_async_copy(near_places.at[side], places.at[side], table_sem.at[side, 0]),
            pltpu.make_async_copy(near_mixes.at[side], mixes.at[side], table_sem.at[side, 1]),
        ]
        for move in moves:
            move.start()
        for move in moves:
            move.wait()

    for side in (0, 1):
        with_neighbour(side, read_near)

    def clear(side):
        def action():
            for c in range(CHUNKS):
                got[c][side] = jnp.zeros((ROWS, GROUP, LANES), jnp.bfloat16)
            for g in range(GROUPS):
                edges[g][side] = jnp.zeros((GROUP, WIDTH), jnp.bfloat16)
                corners[g][side] = jnp.zeros((2, GROUP, TILE), jnp.bfloat16)
            places[side, ENTRIES, ROWS - 1 if side == 0 else 0] = jnp.int32(0)
        pl.when(lat == (0 if side == 0 else n_lat - 1))(action)

    for side in (0, 1):
        clear(side)

    def grow(r, _):
        cells = conc_v[r]
        product = jnp.dot(taps[...], cells, preferred_element_type=jnp.float32)
        total = -sinking * cells.astype(jnp.float32)
        for q in range(4):
            total = total + rates[q, pl.ds(r, 1), :] * product[q * BINS:(q + 1) * BINS]
        base[r] = total
        return 0

    def grow_some(c):
        share = 2 * ROWS // CHUNKS
        if c < CHUNKS // 2:
            lax.fori_loop(c * share, (c + 1) * share, grow, 0, unroll=2)

    def mixed(c, table, r):
        total = None
        for k in range(ENTRIES):
            term = mixes[table, k, r] * held[c][places[table, k, r]].astype(jnp.float32)
            total = term if total is None else total + term
        return total

    def part_copy(c, side, into, there):
        return remote(
            sent[c].at[side], got[c].at[into], part_send.at[c, side], part_recv.at[c, into], lat=there
        )

    def partials(c):
        def action(side, there):
            def one(r, _):
                sent[c][side, r] = mixed(c, side, r).astype(jnp.bfloat16)
                return 0
            lax.fori_loop(0, ROWS, one, 0, unroll=16)
            part_copy(c, side, 1 - side, there).start()
        for side in (0, 1):
            with_neighbour(side, action)

    lane = lax.broadcasted_iota(jnp.int32, (GROUP, TILE), 1)

    def wanted(step):
        return jnp.where(step > -1, step + 1, 0), jnp.where(step < 1, 1 - step, 0)

    def remap(c):
        g, h = c // HALVES, c % HALVES
        for side in (0, 1):
            with_neighbour(side, lambda side, there: part_copy(c, side, side, there).wait_recv())

        def one(r, _):
            total = mixed(c, 2, r)
            for side in (0, 1):
                total = total + mixes[2, ENTRIES + side, r] * got[c][side, r].astype(jnp.float32)
            remapped[g][r, :, pl.ds(h * LANES, LANES)] = total.astype(jnp.bfloat16)
            return 0

        one(0, 0)
        one(ROWS - 1, 0)
        if h == HALVES - 1:
            outer_sends(g, lambda copy: copy.start())
        lax.fori_loop(1, ROWS - 1, one, 0, unroll=10)

    def pack(g):
        first_cells = jnp.zeros((GROUP, TILE), jnp.float32)
        last_cells = first_cells
        for r in range(ROWS):
            before_row, after_row = wanted(places[2, ENTRIES, r])
            start = 4 * r + before_row
            turn = jnp.where(start < TILE, start, 0)
            line = remapped[g][r].astype(jnp.float32)
            first_cells = jnp.where(
                (lane >= start) & (lane < start + after_row), pltpu.roll(line[:, :TILE], turn, 1), first_cells
            )
            last_cells = jnp.where(
                (lane >= 4 * r) & (lane < start), pltpu.roll(line[:, TILE:], turn, 1), last_cells
            )
        packs[g][0] = first_cells.astype(jnp.bfloat16)
        packs[g][1] = last_cells.astype(jnp.bfloat16)

    def halo_copy(g, across, into_across, where):
        return remote(
            packs[g].at[across], halos[g].at[into_across],
            halo_send.at[g, across], halo_recv.at[g, into_across], **where
        )

    def edge_copy(g, side, into, there):
        row = 0 if side == 0 else ROWS - 1
        return remote(
            remapped[g].at[row], edges[g].at[into], edge_send.at[g, side], edge_recv.at[g, into], lat=there
        )

    def corner_copy(g, side, across, into, into_across, where):
        row, first_lane = (0 if side == 0 else ROWS - 1), (0 if across == 0 else WIDTH - TILE)
        return remote(
            remapped[g].at[row, :, pl.ds(first_lane, TILE)], corners[g].at[into, into_across],
            corner_send.at[g, side, across], corner_recv.at[g, into, into_across], **where
        )

    def outer_sends(g, act):
        def action(side, there):
            act(edge_copy(g, side, 1 - side, there))
            for across in (0, 1):
                act(corner_copy(
                    g, side, across, 1 - side, 1 - across, {"lat": there, "lon": beside_lon[across]}
                ))

        for side in (0, 1):
            with_neighbour(side, action)

    def outgoing(g, act):
        for across in (0, 1):
            act(halo_copy(g, across, 1 - across, {"lon": beside_lon[across]}))

    def incoming(g):
        def action(side, there):
            edge_copy(g, side, side, there).wait_recv()
            for across in (0, 1):
                corner_copy(
                    g, side, across, side, across, {"lat": there, "lon": beside_lon[across]}
                ).wait_recv()

        for side in (0, 1):
            with_neighbour(side, action)
        for across in (0, 1):
            halo_copy(g, across, across, {"lon": beside_lon[across]}).wait_recv()

    def shifted(line, halo, turned, step):
        left, right = line[:, :TILE], line[:, TILE:]
        turn = jnp.where(step < 0, step + TILE, step)
        low, high = lane < step, lane >= TILE + step
        halo = pltpu.roll(halo, lax.rem(turn + 2 * TILE - turned, TILE), 1)
        left, right = pltpu.roll(left, turn, 1), pltpu.roll(right, turn, 1)

        def pick(prior, tile, later):
            return jnp.where(low, prior, jnp.where(high, later, tile))

        tiles = pick(halo, left, right), pick(left, right, halo), pick(right, halo, left)
        return jnp.concatenate(tiles, axis=1).astype(jnp.bfloat16)

    def finish(g):
        incoming(g)

        middle = halos[g][0].astype(jnp.float32) + halos[g][1].astype(jnp.float32)

        for side in (0, 1):
            halo = jnp.where(lane < TILE // 2, corners[g][side, 1], corners[g][side, 0]).astype(jnp.float32)
            step = places[side, ENTRIES, ROWS - 1 if side == 0 else 0]
            moved[g][(ROWS + 1) * side] = shifted(edges[g][side].astype(jnp.float32), halo, jnp.int32(0), step)

        def shift(r, _):
            step = places[2, ENTRIES, r]
            moved[g][r + 1] = shifted(remapped[g][r].astype(jnp.float32), middle, 4 * r + wanted(step)[0], step)
            return 0

        lax.fori_loop(0, ROWS, shift, 0, unroll=16)
        bins = pl.ds(g * GROUP, GROUP)

        def block(n, _):
            first = n * BLOCK
            lines = moved[g][pl.ds(first + 1, BLOCK)].reshape(BLOCK * GROUP, 3 * TILE)
            along = jnp.dot(lines, stencil[...], preferred_element_type=jnp.float32)
            for i in range(BLOCK):
                r = first + i
                center, above, below = (
                    moved[g][r + d, :, pl.ds(0, WIDTH)].astype(jnp.float32) for d in (1, 0, 2)
                )
                total = base[r, bins, :] + center
                base[r, bins, :] = total + kappa[pl.ds(r, 1), :] * (
                    (above + below) + along[i * GROUP:(i + 1) * GROUP]
                )
            return 0

        lax.fori_loop(0, ROWS // BLOCK, block, 0)

    def settle_chunk(c):
        remap(c)
        if c % HALVES == HALVES - 1:
            pack(c // HALVES)
            outgoing(c // HALVES, lambda copy: copy.start())

    for c in range(CHUNKS):
        for which in (0, 1):
            raw_arrival(c, which).wait_recv()
        forward(c).start()
        grow_some(c)
        if c >= LAG:
            settle_chunk(c - LAG)
        own_copy(c).wait()
        for which in (2, 3):
            raw_arrival(c, which).wait_recv()
        partials(c)
    finished = 0
    for c in range(CHUNKS - LAG, CHUNKS):
        settle_chunk(c)
        if c < CHUNKS - 1:
            finish(finished)
            finished += 1
    for g in range(finished, GROUPS):
        finish(g)

    for c in range(CHUNKS):
        for copy in raw_sends(c):
            copy.wait_send()
        forward(c).wait_send()
        for side in (0, 1):
            with_neighbour(side, lambda side, there: part_copy(c, side, 1 - side, there).wait_send())
    for g in range(GROUPS):
        outgoing(g, lambda copy: copy.wait_send())
        outer_sends(g, lambda copy: copy.wait_send())

    def dep_sent(side, there):
        for copy in dep_copies(side, 1 - side, there):
            copy.wait_send()

    for side in (0, 1):
        with_neighbour(side, dep_sent)


def solution(mesh):
    n_lat, n_lon = mesh.shape["lat"], mesh.shape["lon"]

    def body(conc, dep_owner, dep_row, dep_weight, dep_count, zonal_offset, agg_rates, toeplitz, settle, kappa):
        owner, row, weight = dep_owner[0].T, dep_row[0].T, dep_weight[0].T
        hbm = pl.BlockSpec(memory_space=pltpu.HBM)
        bf16, f32, i32 = jnp.bfloat16, jnp.float32, jnp.int32
        dma = pltpu.SemaphoreType.DMA
        return pl.pallas_call(
            functools.partial(kernel, n_lat, n_lon),
            out_shape=jax.ShapeDtypeStruct((ROWS, BINS, WIDTH), f32),
            in_specs=[hbm] * 10,
            out_specs=pl.BlockSpec(memory_space=pltpu.VMEM),
            scratch_shapes=[
                pltpu.VMEM((ENTRIES, ROWS), i32),
                pltpu.VMEM((ENTRIES, ROWS), i32),
                pltpu.VMEM((ENTRIES, ROWS), f32),
                pltpu.VMEM((1, ROWS), i32),
                pltpu.VMEM((1, ROWS), i32),
                pltpu.VMEM((4, ROWS, WIDTH), f32),
                pltpu.VMEM((4, 2 * BINS - 1), bf16),
                pltpu.VMEM((1, BINS), f32),
                pltpu.VMEM((ROWS, WIDTH), f32),
                pltpu.VMEM((ROWS, BINS, WIDTH), bf16),
                pltpu.VMEM((4 * BINS, BINS), bf16),
                pltpu.VMEM((4, 2 * BINS), f32),
                pltpu.VMEM((3 * TILE, WIDTH), bf16),
                pltpu.VMEM((3, 8, ROWS), i32),
                pltpu.VMEM((3, 8, ROWS), f32),
                pltpu.VMEM((2, 8, ROWS), i32),
                pltpu.VMEM((2, 8, ROWS), f32),
                pltpu.SMEM((3, 8, ROWS), i32),
                pltpu.SMEM((3, 8, ROWS), f32),
                dma((10,)),
                dma((3, 2)),
            ]
            + [pltpu.VMEM((5 * ROWS, GROUP, LANES), bf16) for _ in range(CHUNKS)]
            + [pltpu.VMEM((2, ROWS, GROUP, LANES), bf16) for _ in range(2 * CHUNKS)]
            + [pltpu.VMEM((ROWS, GROUP, WIDTH), bf16) for _ in range(GROUPS)]
            + [pltpu.VMEM((2, GROUP, TILE), bf16) for _ in range(GROUPS)]
            + [pltpu.VMEM((2, GROUP, TILE), bf16) for _ in range(GROUPS)]
            + [pltpu.VMEM((2, 2, GROUP, TILE), bf16) for _ in range(GROUPS)]
            + [pltpu.VMEM((2, GROUP, WIDTH), bf16) for _ in range(GROUPS)]
            + [pltpu.VMEM((ROWS + 2, GROUP, 3 * TILE), bf16) for _ in range(GROUPS)]
            + [
                dma((2, 2)), dma((2, 2)),
                dma((CHUNKS, 4)), dma((CHUNKS, 4)),
                dma((CHUNKS, 2)), dma((CHUNKS, 2)),
                dma((GROUPS, 2)), dma((GROUPS, 2)),
                dma((GROUPS, 2, 2)), dma((GROUPS, 2, 2)),
                dma((GROUPS, 2)), dma((GROUPS, 2)),
                dma((CHUNKS,)),
            ],
            compiler_params=pltpu.CompilerParams(
                collective_id=0, has_side_effects=True, vmem_limit_bytes=40 << 20
            ),
            name="remap_step",
        )(
            *[
                pltpu.with_memory_space_constraint(operand, pltpu.HBM)
                for operand in (
                    conc, owner, row, weight, dep_count, zonal_offset.reshape(1, ROWS), agg_rates, toeplitz,
                    settle.reshape(1, BINS), kappa,
                )
            ]
        )

    return jax.shard_map(
        body,
        mesh=mesh,
        in_specs=(
            P("lat", None, "lon"),
            P("lon", "lat", None),
            P("lon", "lat", None),
            P("lon", "lat", None),
            P("lon", "lat"),
            P("lat"),
            P(None, "lat", "lon"),
            P(),
            P(),
            P("lat", "lon"),
        ),
        out_specs=P("lat", None, "lon"),
        check_vma=False,
    )
```

```python
import functools

import jax
import jax.numpy as jnp
from jax import lax
from jax.experimental import pallas as pl
from jax.experimental.pallas import tpu as pltpu
from jax.sharding import PartitionSpec as P

MESH = pl.DeviceIdType.MESH
ROWS = 32
BINS = 64
WIDTH = 256
ENTRIES = 4
GROUP = 16
GROUPS = BINS // GROUP
HALVES = 2
LANES = WIDTH // HALVES
CHUNKS = GROUPS * HALVES
BLOCK = 16
AHEAD = 2
LAG = 3
TILE = 128


def kernel(
    n_lat, n_lon,
    conc, owner_h, row_h, weight_h, count_h, offset_h, rates_h, toeplitz_h, settle_h, kappa_h,
    base,
    owner_v, row_v, weight_v, count_v, offset_v, rates, toeplitz, settle, kappa,
    conc_v, taps, toep_v, stencil, places_v, mixes_v, near_places, near_mixes, places, mixes,
    fetch_sem, table_sem,
    *rest,
):
    held = rest[0:CHUNKS]
    sent = rest[CHUNKS:2 * CHUNKS]
    got = rest[2 * CHUNKS:3 * CHUNKS]
    rest = rest[3 * CHUNKS:]
    remapped, packs, halos, corners, edges, moved = (
        rest[i * GROUPS:(i + 1) * GROUPS] for i in range(6)
    )
    (dep_send, dep_recv, raw_send, raw_recv, part_send, part_recv,
     halo_send, halo_recv, corner_send, corner_recv, edge_send, edge_recv, local_sem) = rest[6 * GROUPS:]

    lat = lax.axis_index("lat")
    lon = lax.axis_index("lon")
    core = lax.rem(lon, 2)
    chip = lon - core

    def at_lon(value):
        return lax.rem(value + 2 * n_lon, n_lon)

    sibling = chip + 1 - core
    after = at_lon(chip + 2)
    before = at_lon(chip - 1)
    beside_lon = (at_lon(lon - 1), at_lon(lon + 1))

    def with_neighbour(side, action):
        inside = lat > 0 if side == 0 else lat < n_lat - 1
        pl.when(inside)(functools.partial(action, side, lat - 1 if side == 0 else lat + 1))

    barrier = pltpu.get_barrier_semaphore()
    for step in (-2, -1, 1, 2):
        pl.semaphore_signal(barrier, inc=1, device_id={"lon": at_lon(lon + step)}, device_id_type=MESH)

    def greet(side, there):
        pl.semaphore_signal(barrier, inc=1, device_id={"lat": there}, device_id_type=MESH)
        for across in beside_lon:
            pl.semaphore_signal(barrier, inc=1, device_id={"lat": there, "lon": across}, device_id_type=MESH)

    for side in (0, 1):
        with_neighbour(side, greet)

    fetches = [
        pltpu.make_async_copy(src, dst, fetch_sem.at[i])
        for i, (src, dst) in enumerate([
            (owner_h, owner_v), (row_h, row_v), (weight_h, weight_v), (count_h, count_v), (offset_h, offset_v),
            (toeplitz_h, toeplitz), (settle_h, settle), (rates_h, rates), (kappa_h, kappa), (conc, conc_v),
        ])
    ]
    for fetch in fetches:
        fetch.start()

    def remote(src, dst, send, recv, **where):
        return pltpu.make_async_remote_copy(
            src_ref=src, dst_ref=dst, send_sem=send, recv_sem=recv, device_id=where, device_id_type=MESH
        )

    def window(c):
        g, h = c // HALVES, c % HALVES
        return conc.at[:, pl.ds(g * GROUP, GROUP), pl.ds(h * LANES, LANES)]

    def slot(c, number):
        return held[c].at[pl.ds(number * ROWS, ROWS)]

    single_to = jnp.where(core == 0, after, before)
    double_to = jnp.where(core == 0, before, after)

    def single_send(c):
        return remote(window(c), slot(c, 4 * core), raw_send.at[c, 0], raw_recv.at[c, 0], lon=single_to)

    def double_send(c):
        return remote(window(c), slot(c, 3 - 2 * core), raw_send.at[c, 1], raw_recv.at[c, 1], lon=double_to)

    def sibling_send(c):
        return remote(window(c), slot(c, 1 + 2 * core), raw_send.at[c, 2], raw_recv.at[c, 2], lon=sibling)

    def raw_arrival(c, kind):
        number = (4 * core, 1 + 2 * core, 3 - 2 * core, 4 - 4 * core)[kind]
        return remote(window(c), slot(c, number), raw_send.at[c, 3], raw_recv.at[c, kind], lon=sibling)

    def forward(c):
        return remote(
            slot(c, 1 + 2 * core), slot(c, 4 * core), raw_send.at[c, 3], raw_recv.at[c, 3], lon=sibling
        )

    def own_copy(c):
        return pltpu.make_async_copy(window(c), slot(c, 2), local_sem.at[c])

    def dep_copies(side, into, there):
        return [
            remote(places_v.at[side], near_places.at[into], dep_send.at[side, 0], dep_recv.at[into, 0], lat=there),
            remote(mixes_v.at[side], near_mixes.at[into], dep_send.at[side, 1], dep_recv.at[into, 1], lat=there),
        ]

    def dep_start(side, there):
        for copy in dep_copies(side, 1 - side, there):
            copy.start()

    pl.semaphore_wait(barrier, 4 + 3 * (jnp.where(lat > 0, 1, 0) + jnp.where(lat < n_lat - 1, 1, 0)))
    for c in range(CHUNKS):
        double_send(c).start()
        if c < AHEAD:
            single_send(c).start()
        sibling_send(c).start()
    for c in range(CHUNKS):
        own_copy(c).start()

    for fetch in fetches[:5]:
        fetch.wait()
    owner, weight = owner_v[...], weight_v[...]
    live = lax.broadcasted_iota(jnp.int32, (ENTRIES, ROWS), 0) < count_v[...]
    places_v[...] = jnp.zeros_like(places_v)
    mixes_v[...] = jnp.zeros_like(mixes_v)
    for group, table in ((0, 0), (2, 1), (1, 2)):
        mine = live & (owner >= 5 * group) & (owner < 5 * group + 5)
        mass = jnp.where(mine, weight, 0.0)
        places_v[table, pl.ds(0, ENTRIES), :] = jnp.where(mine, (owner - 5 * group) * ROWS + row_v[...], 2 * ROWS)
        places_v[table, pl.ds(ENTRIES, 1), :] = offset_v[...]
        if group != 1:
            single = jnp.sum(mine.astype(jnp.int32), axis=0, keepdims=True) == 1
            mixes_v[2, pl.ds(ENTRIES + table, 1), :] = jnp.where(single, jnp.sum(mass, axis=0, keepdims=True), 1.0)
            mass = jnp.where(mine & single, 1.0, mass)
        mixes_v[table, pl.ds(0, ENTRIES), :] = mass
    own_tables = [
        pltpu.make_async_copy(places_v.at[2], places.at[2], table_sem.at[2, 0]),
        pltpu.make_async_copy(mixes_v.at[2], mixes.at[2], table_sem.at[2, 1]),
    ]
    for move in own_tables:
        move.start()

    for side in (0, 1):
        with_neighbour(side, dep_start)
    for fetch in fetches[5:]:
        fetch.wait()
    toep_v[...] = jnp.zeros_like(toep_v)
    toep_v[:, pl.ds(0, 2 * BINS - 1)] = toeplitz[...].astype(jnp.float32)
    for q in range(4):
        line = jnp.broadcast_to(toep_v[pl.ds(q, 1), :], (2 * BINS, 2 * BINS))
        turned = pltpu.roll(line, BINS + 1, 1, stride=1, stride_axis=0)
        taps[pl.ds(q * BINS, BINS), :] = turned.T[:BINS, :BINS].astype(jnp.bfloat16)
    diagonal = lax.broadcasted_iota(jnp.int32, (BINS, BINS), 0) == lax.broadcasted_iota(jnp.int32, (BINS, BINS), 1)
    sinking = jnp.sum(jnp.where(diagonal, jnp.broadcast_to(settle[...], (BINS, BINS)), 0.0), axis=1, keepdims=True)
    sinking = jnp.broadcast_to(sinking, (BINS, WIDTH))

    apart = lax.broadcasted_iota(jnp.int32, (3 * TILE, WIDTH), 0) - lax.broadcasted_iota(
        jnp.int32, (3 * TILE, WIDTH), 1
    )
    near = (apart == 1) | (apart == -1) | (apart == 3 * TILE - 1)
    stencil[...] = jnp.where(near, 1.0, jnp.where(apart == 0, -4.0, 0.0)).astype(jnp.bfloat16)

    for move in own_tables:
        move.wait()

    def read_near(side, there):
        for copy in dep_copies(side, side, there):
            copy.wait_recv()
        moves = [
            pltpu.make_async_copy(near_places.at[side], places.at[side], table_sem.at[side, 0]),
            pltpu.make_async_copy(near_mixes.at[side], mixes.at[side], table_sem.at[side, 1]),
        ]
        for move in moves:
            move.start()
        for move in moves:
            move.wait()

    for side in (0, 1):
        with_neighbour(side, read_near)

    def clear(side):
        def action():
            for c in range(CHUNKS):
                got[c][side] = jnp.zeros((ROWS, GROUP, LANES), jnp.bfloat16)
            for g in range(GROUPS):
                edges[g][side] = jnp.zeros((GROUP, WIDTH), jnp.bfloat16)
                corners[g][side] = jnp.zeros((2, GROUP, TILE), jnp.bfloat16)
            places[side, ENTRIES, ROWS - 1 if side == 0 else 0] = jnp.int32(0)
        pl.when(lat == (0 if side == 0 else n_lat - 1))(action)

    for side in (0, 1):
        clear(side)

    def grow(r, _):
        cells = conc_v[r]
        product = jnp.dot(taps[...], cells, preferred_element_type=jnp.float32)
        total = -sinking * cells.astype(jnp.float32)
        for q in range(4):
            total = total + rates[q, pl.ds(r, 1), :] * product[q * BINS:(q + 1) * BINS]
        base[r] = total
        return 0

    def grow_some(c):
        share = 2 * ROWS // CHUNKS
        if c < CHUNKS // 2:
            lax.fori_loop(c * share, (c + 1) * share, grow, 0, unroll=8)

    def mixed(c, table, r):
        total = None
        for k in range(ENTRIES):
            term = mixes[table, k, r] * held[c][places[table, k, r]].astype(jnp.float32)
            total = term if total is None else total + term
        return total

    def part_copy(c, side, into, there):
        return remote(
            sent[c].at[side], got[c].at[into], part_send.at[c, side], part_recv.at[c, into], lat=there
        )

    def partials(c):
        def action(side, there):
            def one(r, _):
                sent[c][side, r] = mixed(c, side, r).astype(jnp.bfloat16)
                return 0
            lax.fori_loop(0, ROWS, one, 0, unroll=16)
            part_copy(c, side, 1 - side, there).start()
        for side in (0, 1):
            with_neighbour(side, action)

    lane = lax.broadcasted_iota(jnp.int32, (GROUP, TILE), 1)

    def wanted(step):
        return jnp.where(step > -1, step + 1, 0), jnp.where(step < 1, 1 - step, 0)

    def remap(c):
        g, h = c // HALVES, c % HALVES
        for side in (0, 1):
            with_neighbour(side, lambda side, there: part_copy(c, side, side, there).wait_recv())

        def one(r, _):
            total = mixed(c, 2, r)
            for side in (0, 1):
                total = total + mixes[2, ENTRIES + side, r] * got[c][side, r].astype(jnp.float32)
            remapped[g][r, :, pl.ds(h * LANES, LANES)] = total.astype(jnp.bfloat16)
            return 0

        one(0, 0)
        one(ROWS - 1, 0)
        if h == HALVES - 1:
            outer_sends(g, lambda copy: copy.start())
        lax.fori_loop(1, ROWS - 1, one, 0, unroll=10)

    def pack(g):
        first_cells = jnp.zeros((GROUP, TILE), jnp.float32)
        last_cells = first_cells
        for r in range(ROWS):
            before_row, after_row = wanted(places[2, ENTRIES, r])
            start = 4 * r + before_row
            turn = jnp.where(start < TILE, start, 0)
            line = remapped[g][r].astype(jnp.float32)
            first_cells = jnp.where(
                (lane >= start) & (lane < start + after_row), pltpu.roll(line[:, :TILE], turn, 1), first_cells
            )
            last_cells = jnp.where(
                (lane >= 4 * r) & (lane < start), pltpu.roll(line[:, TILE:], turn, 1), last_cells
            )
        packs[g][0] = first_cells.astype(jnp.bfloat16)
        packs[g][1] = last_cells.astype(jnp.bfloat16)

    def halo_copy(g, across, into_across, where):
        return remote(
            packs[g].at[across], halos[g].at[into_across],
            halo_send.at[g, across], halo_recv.at[g, into_across], **where
        )

    def edge_copy(g, side, into, there):
        row = 0 if side == 0 else ROWS - 1
        return remote(
            remapped[g].at[row], edges[g].at[into], edge_send.at[g, side], edge_recv.at[g, into], lat=there
        )

    def corner_copy(g, side, across, into, into_across, where):
        row, first_lane = (0 if side == 0 else ROWS - 1), (0 if across == 0 else WIDTH - TILE)
        return remote(
            remapped[g].at[row, :, pl.ds(first_lane, TILE)], corners[g].at[into, into_across],
            corner_send.at[g, side, across], corner_recv.at[g, into, into_across], **where
        )

    def outer_sends(g, act):
        def action(side, there):
            act(edge_copy(g, side, 1 - side, there))
            for across in (0, 1):
                act(corner_copy(
                    g, side, across, 1 - side, 1 - across, {"lat": there, "lon": beside_lon[across]}
                ))

        for side in (0, 1):
            with_neighbour(side, action)

    def outgoing(g, act):
        for across in (0, 1):
            act(halo_copy(g, across, 1 - across, {"lon": beside_lon[across]}))

    def incoming(g):
        def action(side, there):
            edge_copy(g, side, side, there).wait_recv()
            for across in (0, 1):
                corner_copy(
                    g, side, across, side, across, {"lat": there, "lon": beside_lon[across]}
                ).wait_recv()

        for side in (0, 1):
            with_neighbour(side, action)
        for across in (0, 1):
            halo_copy(g, across, across, {"lon": beside_lon[across]}).wait_recv()

    def shifted(line, halo, turned, step):
        left, right = line[:, :TILE], line[:, TILE:]
        turn = jnp.where(step < 0, step + TILE, step)
        low, high = lane < step, lane >= TILE + step
        halo = pltpu.roll(halo, lax.rem(turn + 2 * TILE - turned, TILE), 1)
        left, right = pltpu.roll(left, turn, 1), pltpu.roll(right, turn, 1)

        def pick(prior, tile, later):
            return jnp.where(low, prior, jnp.where(high, later, tile))

        tiles = pick(halo, left, right), pick(left, right, halo), pick(right, halo, left)
        return jnp.concatenate(tiles, axis=1).astype(jnp.bfloat16)

    def finish(g):
        incoming(g)

        middle = halos[g][0].astype(jnp.float32) + halos[g][1].astype(jnp.float32)

        for side in (0, 1):
            halo = jnp.where(lane < TILE // 2, corners[g][side, 1], corners[g][side, 0]).astype(jnp.float32)
            step = places[side, ENTRIES, ROWS - 1 if side == 0 else 0]
            moved[g][(ROWS + 1) * side] = shifted(edges[g][side].astype(jnp.float32), halo, jnp.int32(0), step)

        def shift(r, _):
            step = places[2, ENTRIES, r]
            moved[g][r + 1] = shifted(remapped[g][r].astype(jnp.float32), middle, 4 * r + wanted(step)[0], step)
            return 0

        lax.fori_loop(0, ROWS, shift, 0, unroll=16)
        bins = pl.ds(g * GROUP, GROUP)

        def block(n, _):
            first = n * BLOCK
            lines = moved[g][pl.ds(first + 1, BLOCK)].reshape(BLOCK * GROUP, 3 * TILE)
            along = jnp.dot(lines, stencil[...], preferred_element_type=jnp.float32)
            for i in range(BLOCK):
                r = first + i
                center, above, below = (
                    moved[g][r + d, :, pl.ds(0, WIDTH)].astype(jnp.float32) for d in (1, 0, 2)
                )
                total = base[r, bins, :] + center
                base[r, bins, :] = total + kappa[pl.ds(r, 1), :] * (
                    (above + below) + along[i * GROUP:(i + 1) * GROUP]
                )
            return 0

        lax.fori_loop(0, ROWS // BLOCK, block, 0)

    def settle_chunk(c):
        remap(c)
        if c % HALVES == HALVES - 1:
            pack(c // HALVES)
            outgoing(c // HALVES, lambda copy: copy.start())

    for c in range(CHUNKS):
        raw_arrival(c, 1).wait_recv()
        forward(c).start()
        grow_some(c)
        if c >= LAG:
            settle_chunk(c - LAG)
        own_copy(c).wait()
        raw_arrival(c, 0).wait_recv()
        if c + AHEAD < CHUNKS:
            single_send(c + AHEAD).start()
        for kind in (2, 3):
            raw_arrival(c, kind).wait_recv()
        partials(c)
    for c in range(CHUNKS - LAG, CHUNKS):
        settle_chunk(c)
        if c == CHUNKS - 2:
            finish(0)
    for g in range(1, GROUPS):
        finish(g)

    for c in range(CHUNKS):
        for copy in (single_send(c), double_send(c), sibling_send(c)):
            copy.wait_send()
        forward(c).wait_send()
        for side in (0, 1):
            with_neighbour(side, lambda side, there: part_copy(c, side, 1 - side, there).wait_send())
    for g in range(GROUPS):
        outgoing(g, lambda copy: copy.wait_send())
        outer_sends(g, lambda copy: copy.wait_send())

    def dep_sent(side, there):
        for copy in dep_copies(side, 1 - side, there):
            copy.wait_send()

    for side in (0, 1):
        with_neighbour(side, dep_sent)


def solution(mesh):
    n_lat, n_lon = mesh.shape["lat"], mesh.shape["lon"]

    def body(conc, dep_owner, dep_row, dep_weight, dep_count, zonal_offset, agg_rates, toeplitz, settle, kappa):
        owner, row, weight = dep_owner[0].T, dep_row[0].T, dep_weight[0].T
        hbm = pl.BlockSpec(memory_space=pltpu.HBM)
        bf16, f32, i32 = jnp.bfloat16, jnp.float32, jnp.int32
        dma = pltpu.SemaphoreType.DMA
        return pl.pallas_call(
            functools.partial(kernel, n_lat, n_lon),
            out_shape=jax.ShapeDtypeStruct((ROWS, BINS, WIDTH), f32),
            in_specs=[hbm] * 10,
            out_specs=pl.BlockSpec(memory_space=pltpu.VMEM),
            scratch_shapes=[
                pltpu.VMEM((ENTRIES, ROWS), i32),
                pltpu.VMEM((ENTRIES, ROWS), i32),
                pltpu.VMEM((ENTRIES, ROWS), f32),
                pltpu.VMEM((1, ROWS), i32),
                pltpu.VMEM((1, ROWS), i32),
                pltpu.VMEM((4, ROWS, WIDTH), f32),
                pltpu.VMEM((4, 2 * BINS - 1), bf16),
                pltpu.VMEM((1, BINS), f32),
                pltpu.VMEM((ROWS, WIDTH), f32),
                pltpu.VMEM((ROWS, BINS, WIDTH), bf16),
                pltpu.VMEM((4 * BINS, BINS), bf16),
                pltpu.VMEM((4, 2 * BINS), f32),
                pltpu.VMEM((3 * TILE, WIDTH), bf16),
                pltpu.VMEM((3, 8, ROWS), i32),
                pltpu.VMEM((3, 8, ROWS), f32),
                pltpu.VMEM((2, 8, ROWS), i32),
                pltpu.VMEM((2, 8, ROWS), f32),
                pltpu.SMEM((3, 8, ROWS), i32),
                pltpu.SMEM((3, 8, ROWS), f32),
                dma((10,)),
                dma((3, 2)),
            ]
            + [pltpu.VMEM((5 * ROWS, GROUP, LANES), bf16) for _ in range(CHUNKS)]
            + [pltpu.VMEM((2, ROWS, GROUP, LANES), bf16) for _ in range(2 * CHUNKS)]
            + [pltpu.VMEM((ROWS, GROUP, WIDTH), bf16) for _ in range(GROUPS)]
            + [pltpu.VMEM((2, GROUP, TILE), bf16) for _ in range(GROUPS)]
            + [pltpu.VMEM((2, GROUP, TILE), bf16) for _ in range(GROUPS)]
            + [pltpu.VMEM((2, 2, GROUP, TILE), bf16) for _ in range(GROUPS)]
            + [pltpu.VMEM((2, GROUP, WIDTH), bf16) for _ in range(GROUPS)]
            + [pltpu.VMEM((ROWS + 2, GROUP, 3 * TILE), bf16) for _ in range(GROUPS)]
            + [
                dma((2, 2)), dma((2, 2)),
                dma((CHUNKS, 4)), dma((CHUNKS, 4)),
                dma((CHUNKS, 2)), dma((CHUNKS, 2)),
                dma((GROUPS, 2)), dma((GROUPS, 2)),
                dma((GROUPS, 2, 2)), dma((GROUPS, 2, 2)),
                dma((GROUPS, 2)), dma((GROUPS, 2)),
                dma((CHUNKS,)),
            ],
            compiler_params=pltpu.CompilerParams(
                collective_id=0, has_side_effects=True, vmem_limit_bytes=40 << 20
            ),
            name="remap_step",
        )(
            *[
                pltpu.with_memory_space_constraint(operand, pltpu.HBM)
                for operand in (
                    conc, owner, row, weight, dep_count, zonal_offset.reshape(1, ROWS), agg_rates, toeplitz,
                    settle.reshape(1, BINS), kappa,
                )
            ]
        )

    return jax.shard_map(
        body,
        mesh=mesh,
        in_specs=(
            P("lat", None, "lon"),
            P("lon", "lat", None),
            P("lon", "lat", None),
            P("lon", "lat", None),
            P("lon", "lat"),
            P("lat"),
            P(None, "lat", "lon"),
            P(),
            P(),
            P("lat", "lon"),
        ),
        out_specs=P("lat", None, "lon"),
        check_vma=False,
    )
```
